128 devices in a mesh: tm: 16 (over z_lo, y, core), head: 8 (over z_hi, x).
Axes of the slice: x: 4, y: 4, z: 4 (z_hi: 2, z_lo: 2; z = z_hi * 2 + z_lo), core: 2. Of those that a mesh axis runs over, the one named last changes fastest.
Arguments:
- query_vectors: bfloat16 [16384, 4096], P('tm', 'head'), may hold values from -6 to 6
- key_vectors: bfloat16 [16384, 4096], P('tm', 'head'), may hold values from -0.125 to 0.125
- value_vectors: bfloat16 [16384, 4096], P('tm', 'head'), may hold values from -6 to 6
- grad_out: bfloat16 [16384, 4096], P('tm', 'head'), may hold values from -8 to 8
- out_weight: bfloat16 [4096, 4096], P('tm', 'head'), may hold values from -0.09375 to 0.09375
- periods: int32 [32], P('head'), may hold values from 1 to 128, as said below
- log_decay: float32 [32, 16384], P('head', 'tm'), may hold values from -0.1109375 to 0, as said below
Outputs:
- query_gradient: bfloat16 [16384, 4096], P('tm', 'head')
- key_gradient: bfloat16 [16384, 4096], P('tm', 'head')
- value_gradient: bfloat16 [16384, 4096], P('tm', 'head')
- grad_weight: float32 [4096, 4096], P('tm', 'head')
The draws below stay inside these ranges and needn't reach their ends.
Inputs may be any that keep to these rules, and one draw needn't show every extreme that they name: `periods`: some head has period 1 and some head period 128. `log_decay`: Negative.
All inputs are finite; a program needn't handle non-finite values.
Results may differ from the reference program's by a relative error of at most 0.023.
Values may be sent and summed in bfloat16 or wider, within the bound.
A program may use at most 128 MiB of HBM per device.

```python
import math
import jax
import jax.numpy as jnp
from jax import lax

D = 4096
H = 32
DK = 128
BLK = 512
TOK_DEV = 1024
TOKENS = 16384


def draw_periods(key, part):
    base_key = jax.random.fold_in(key, 11)
    first_key, second_key = jax.random.split(base_key)
    periods = jax.random.randint(first_key, (H,), 1, 129)
    shuffled = jax.random.permutation(second_key, H)
    periods = periods.at[shuffled[0]].set(1)
    periods = periods.at[shuffled[1]].set(128)
    return periods.astype(jnp.int32)


def draw_log_decay(key, part):
    base_key = jax.random.fold_in(key, 23)
    split_keys = jax.random.split(base_key, 7)
    rapid_share = 0.5
    rapid = jax.random.uniform(split_keys[0], (H,)) < rapid_share
    span_len = jax.random.uniform(split_keys[1], (H,), minval=30.0, maxval=50.0)
    slow_rate = jax.random.uniform(split_keys[2], (H,), minval=0.05, maxval=0.25) * math.log(10.0) / TOKENS
    decay_factor = jnp.where(rapid, 1.0 / span_len, slow_rate)
    decay_spread = jax.random.uniform(split_keys[3], (H, TOKENS), minval=0.5, maxval=1.5)
    period_region = 2.0 ** jax.random.uniform(split_keys[4], (H, TOKENS // TOK_DEV), minval=-1.0, maxval=1.0)
    period_region = jnp.repeat(period_region, TOK_DEV, axis=1)
    window = min(128, TOKENS)
    starts = jax.random.randint(split_keys[5], (H, 2), 0, TOKENS - window + 1)
    decay_strength = jnp.log(jax.random.uniform(split_keys[6], (H, 2), minval=0.5, maxval=0.8)) / window
    positions = jnp.arange(TOKENS)
    inner_block = (positions[None, None, :] >= starts[:, :, None]) & (positions[None, None, :] < starts[:, :, None] + window)
    period_groups = jnp.sum(inner_block.astype(jnp.float32) * decay_strength[:, :, None], axis=1)
    return (-decay_factor[:, None] * decay_spread * period_region + period_groups).astype(jnp.float32)


def strengthened(entries, stream_key, source, target, parts, factor):
    owner, partner = [(jnp.arange(entries.shape[dim]) // (entries.shape[dim] // parts)).reshape([-1 if axis == dim else 1 for axis in range(entries.ndim)]) for dim in (source, target)]
    chosen = jax.random.permutation(stream_key, parts)[partner]
    strong = (owner == chosen) | (owner == (partner + parts // 2) % parts)
    return jnp.where(strong, factor * entries, entries)


def block_scale(stream_key, dims, pieces, least, top_value):
    def one(dim, parts):
        draws = jax.random.uniform(jax.random.fold_in(jax.random.fold_in(stream_key, 6), dim), (parts,), jnp.float32, least / len(pieces), top_value / len(pieces))
        return jnp.repeat(jnp.exp(draws), dims[dim] // parts).reshape((-1,) + (1,) * (len(dims) - dim - 1))

    level = one(*pieces[0])
    for cut in pieces[1:]:
        level = level * one(*cut)
    return level


def scatter_about(own_key, shape, scale, limit, pieces=(), held_as=jnp.bfloat16):
    entries = scale * jax.random.normal(own_key, shape, jnp.float32)
    if pieces:
        entries = entries * block_scale(own_key, shape, pieces, -0.22, 0.18)
    return jnp.clip(entries, -limit, limit).astype(held_as)


def bell_draw_with(rng, extent, width, most, pieces, heavy, kind=jnp.bfloat16):
    values = width * jax.random.normal(rng, extent, jnp.float32)
    if pieces:
        values = values * block_scale(rng, extent, pieces, -0.22, 0.18)
    return jnp.clip(strengthened(values, jax.random.fold_in(rng, 3), *heavy), -most, most).astype(kind)


def setup_inputs(seed: int = 0) -> dict:
    splits = jax.random.split(jax.random.key(seed), 8)
    return {
        "query_vectors": scatter_about(splits[0], (TOKENS, H * DK), 1.0, 6.0, ((0, 16), (1, 8))),
        "key_vectors": scatter_about(splits[1], (TOKENS, H * DK), 0.02, 0.125, ((0, 16), (1, 8))),
        "value_vectors": scatter_about(splits[2], (TOKENS, H * DK), 1.0, 6.0, ((0, 16), (1, 8))),
        "grad_out": bell_draw_with(splits[3], (TOKENS, D), 1.0, 8.0, ((0, 16), (1, 8)), (0, 1, 16, 2.0)),
        "out_weight": scatter_about(splits[4], (D, H * DK), D ** -0.5, 0.09375, ((0, 16), (1, 8))),
        "periods": draw_periods(jax.random.fold_in(splits[7], 71), 0),
        "log_decay": draw_log_decay(jax.random.fold_in(splits[7], 71), 0),
    }


def to_single_precision(tensor):
    return tensor.astype(jnp.float32)


def block_mask(cumul, update):
    span_len = cumul.shape[1]
    causal = jnp.arange(span_len)[:, None] >= jnp.arange(span_len)[None, :]
    spread = jnp.where(causal[None], cumul[:, :, None] - cumul[:, None, :], -jnp.inf)
    return jnp.exp(spread) * update[:, None, :]


def reference(query_vectors, key_vectors, value_vectors, grad_out, out_weight, periods, log_decay):
    grad_mixed = jnp.dot(grad_out, out_weight, preferred_element_type=jnp.float32).astype(jnp.bfloat16)
    positions = jnp.arange(TOKENS, dtype=jnp.int32)
    update = (positions[None, :] % periods[:, None] == 0).astype(jnp.float32)
    step_log = update * periods[:, None].astype(jnp.float32) * log_decay
    block_count = TOKENS // BLK
    cumulative = jnp.cumsum(step_log.reshape(H, block_count, BLK), axis=2).transpose(1, 0, 2)
    updates = update.reshape(H, block_count, BLK).transpose(1, 0, 2)

    def blocked(tensor):
        return tensor.reshape(block_count, BLK, H, DK)

    query_blocks = blocked(query_vectors)
    key_blocks = blocked(key_vectors)
    value_blocks = blocked(value_vectors)
    grad_blocks = blocked(grad_mixed)
    zero_state = jnp.zeros((H, DK, DK), jnp.float32)

    def forward(running, section):
        key_matrix, value_matrix, cumul, update_rows = section
        block_total = cumul[:, -1]
        factor = update_rows * jnp.exp(block_total[:, None] - cumul)
        decay_scaled = (to_single_precision(key_matrix) * factor.T[:, :, None]).astype(jnp.bfloat16)
        outer_product = jnp.einsum('ptz,ptb->tzb', to_single_precision(decay_scaled), to_single_precision(value_matrix))
        return jnp.exp(block_total)[:, None, None] * running + outer_product, running

    _, starts = lax.scan(forward, zero_state, (key_blocks, value_blocks, cumulative, updates))

    def backward(carried_in, section):
        query_matrix, gradient_rows, cumul = section
        decay_scaled = (to_single_precision(query_matrix) * jnp.exp(cumul).T[:, :, None]).astype(jnp.bfloat16)
        outer_product = jnp.einsum('yop,yoj->opj', to_single_precision(decay_scaled), to_single_precision(gradient_rows))
        return jnp.exp(cumul[:, -1])[:, None, None] * carried_in + outer_product, carried_in

    _, finishes = lax.scan(backward, zero_state, (query_blocks, grad_blocks, cumulative), reverse=True)

    def every_output(section):
        query_matrix, key_matrix, value_matrix, gradient_rows, cumul, update_rows, state_start, finish = section
        decay_mask = block_mask(cumul, update_rows)
        scores = jnp.einsum('thk,shk->hts', to_single_precision(query_matrix), to_single_precision(key_matrix))
        reversed_blocks = jnp.einsum('thv,shv->hts', to_single_precision(gradient_rows), to_single_precision(value_matrix))
        projection_weight = (scores * decay_mask).astype(jnp.bfloat16)
        reversed_blocks = (reversed_blocks * decay_mask).astype(jnp.bfloat16)
        state_reduced = state_start.astype(jnp.bfloat16)
        carry_reduced = finish.astype(jnp.bfloat16)
        incoming_gradient = jnp.exp(cumul).T[:, :, None]
        outgoing_gradient = (update_rows * jnp.exp(cumul[:, -1][:, None] - cumul)).T[:, :, None]
        within = jnp.einsum('hts,shv->thv', to_single_precision(projection_weight), to_single_precision(value_matrix))
        carried_state = jnp.einsum('qml,mla->qma', to_single_precision(query_matrix), to_single_precision(state_reduced))
        mixed = (within + incoming_gradient * carried_state).astype(jnp.bfloat16)
        query_gradient = jnp.einsum('gea,agq->egq', to_single_precision(reversed_blocks), to_single_precision(key_matrix)) + incoming_gradient * jnp.einsum('sba,bda->sbd', to_single_precision(gradient_rows), to_single_precision(state_reduced))
        key_gradient = jnp.einsum('rwy,wre->yre', to_single_precision(reversed_blocks), to_single_precision(query_matrix)) + outgoing_gradient * jnp.einsum('wqx,qgx->wqg', to_single_precision(value_matrix), to_single_precision(carry_reduced))
        value_gradient = jnp.einsum('kyp,ykb->pkb', to_single_precision(projection_weight), to_single_precision(gradient_rows)) + outgoing_gradient * jnp.einsum('imx,mxd->imd', to_single_precision(key_matrix), to_single_precision(carry_reduced))
        return mixed, query_gradient.astype(jnp.bfloat16), key_gradient.astype(jnp.bfloat16), value_gradient.astype(jnp.bfloat16)

    sections = (query_blocks, key_blocks, value_blocks, grad_blocks, cumulative, updates, starts, finishes)
    mixed, query_gradient, key_gradient, value_gradient = lax.map(every_output, sections)
    mixed = mixed.reshape(TOKENS, H * DK)
    grad_weight = jnp.dot(grad_out.T, mixed, preferred_element_type=jnp.float32)
    return (query_gradient.reshape(TOKENS, H * DK), key_gradient.reshape(TOKENS, H * DK), value_gradient.reshape(TOKENS, H * DK), grad_weight)
```

```python
import jax
import jax.numpy as jnp
from jax import lax
from jax.experimental import pallas as pl
from jax.experimental.pallas import tpu as pltpu
from jax.sharding import PartitionSpec as P

DK = 128
BLK = 512
NH = 4
TM = 16
ROWS = 1024
HALF = 256
BF = jnp.bfloat16
F32 = jnp.float32
MESH = pl.DeviceIdType.MESH


def mm(a, b):
    return jnp.dot(a, b, preferred_element_type=F32)


def mm_nt(a, b):
    return lax.dot_general(a, b, (((1,), (1,)), ((), ())), preferred_element_type=F32)


def mm_tn(a, b):
    return lax.dot_general(a, b, (((0,), (0,)), ((), ())), preferred_element_type=F32)


def column(row):
    return jnp.transpose(jnp.broadcast_to(row, (DK, row.shape[1])))


def kernel(
    per_ref,
    ld_ref,
    q_hbm,
    k_hbm,
    v_hbm,
    g_hbm,
    w_hbm,
    dq_ref,
    dk_ref,
    dv_ref,
    gw_ref,
    q,
    k,
    v,
    e,
    grads,
    weight,
    acc,
    cum,
    upd,
    fcol,
    ecol,
    mask,
    wts,
    qst,
    mixt,
    st,
    sb,
    rl,
    dvp,
    tx_s,
    rx_s,
    tx_p,
    rx_p,
    tx_r,
    rx_r,
    tx_o,
    rx_o,
    dec,
    pair_tx,
    pair_rx,
    pair_own,
    y_tx,
    y_rx,
    z_tx,
    z_rx,
    load_sem,
    ag_send,
    ag_recv,
    w_send,
    w_recv,
    s_send,
    s_recv,
    c_send,
    c_recv,
    y_send,
    y_recv,
    z_send,
    z_recv,
):
    tm = lax.axis_index("tm")
    hd = lax.axis_index("head")
    x = lax.rem(hd, 4)
    zh = hd // 4
    right = zh * 4 + lax.rem(x + 1, 4)
    left = zh * 4 + lax.rem(x + 3, 4)
    far = zh * 4 + lax.rem(x + 2, 4)
    across = lax.rem(hd + 4, 8)
    core = lax.rem(tm, 2)
    y = lax.rem(tm // 2, 4)
    zl = tm // 8
    mate = tm + 1 - 2 * core

    def tm_at(zl_, y_, core_):
        return (zl_ * 4 + y_) * 2 + core_

    def local(src, dst, i):
        return pltpu.make_async_copy(src, dst, load_sem.at[i])

    loads = [
        local(q_hbm, q, 0),
        local(k_hbm, k, 1),
        local(v_hbm, v, 2),
        local(g_hbm, grads.at[hd], 3),
        local(w_hbm, weight.at[tm // 2, pl.ds(core * HALF, HALF)], 4),
    ]
    for item in loads:
        item.start()

    barrier = pltpu.get_barrier_semaphore()
    for d in range(1, TM):
        pl.semaphore_signal(
            barrier, inc=1, device_id={"tm": lax.rem(tm + d, TM)}, device_id_type=MESH
        )
    for peer in (right, left, across):
        pl.semaphore_signal(barrier, inc=1, device_id={"head": peer}, device_id_type=MESH)
    pl.semaphore_wait(barrier, TM + 2)

    sent = []

    def send(src, dst, send_sem, recv_sem, device):
        copy = pltpu.make_async_remote_copy(
            src_ref=src,
            dst_ref=dst,
            send_sem=send_sem,
            recv_sem=recv_sem,
            device_id=device,
            device_id_type=MESH,
        )
        copy.start()
        sent.append(copy)
        return copy

    def gather(src, slot, first, count, peer, n):
        rows = pl.ds(first, count)
        return send(
            src.at[rows],
            grads.at[slot, rows],
            ag_send.at[n],
            ag_recv.at[n],
            {"head": peer},
        )

    to_right = [gather(g_hbm, hd, c * 512, 512, right, c) for c in range(2)]
    to_left = [gather(g_hbm, hd, c * 512, 512, left, 2 + c) for c in range(2)]
    to_across = [gather(g_hbm, hd, 0, 512, across, 4)]

    def w_copy(src, owner, device, n):
        return send(
            src,
            weight.at[owner // 2, pl.ds(lax.rem(owner, 2) * HALF, HALF)],
            w_send.at[n],
            w_recv.at[n],
            {"tm": device},
        )

    def w_block(owner):
        return weight.at[owner // 2, pl.ds(lax.rem(owner, 2) * HALF, HALF)]

    ids = lax.broadcasted_iota(jnp.int32, (8, BLK), 0)
    lane = lax.broadcasted_iota(jnp.int32, (8, BLK), 1)
    head_of = lax.rem(ids, NH)
    period = jnp.full((8, BLK), per_ref[0], jnp.int32)
    for h in range(1, NH):
        period = jnp.where(head_of == h, per_ref[h], period)
    period = period.astype(F32)
    pos = (tm * ROWS + (ids // NH) * BLK + lane).astype(F32)
    turns = jnp.floor((pos + 0.5) * (1.0 / period))
    update = jnp.where(pos == turns * period, 1.0, 0.0).astype(F32)
    cum[0:NH, :] = ld_ref[:, 0:BLK]
    cum[NH : 2 * NH, :] = ld_ref[:, BLK : 2 * BLK]
    run = update * period * cum[...]
    shift = 1
    while shift < BLK:
        run = run + jnp.where(lane >= shift, pltpu.roll(run, shift, axis=1), 0.0)
        shift *= 2
    cum[...] = run
    upd[...] = update

    def rows_of(p):
        return cum[pl.ds(p, 1), :], upd[pl.ds(p, 1), :]

    def total_of(p):
        row = cum[pl.ds(p, 1), :]
        return jnp.broadcast_to(row[:, BLK - 1 : BLK], (1, DK))

    def cols(h):
        return pl.ds(pl.multiple_of(h * DK, DK), DK)

    for i in range(3):
        loads[i].wait()

    @pl.loop(0, NH)
    def _(h):
        for b in range(2):
            p = b * NH + h
            row, urow = rows_of(p)
            factor = column(urow * jnp.exp(row[:, BLK - 1 : BLK] - row))
            fcol[p] = factor
            scaled = (k[b * BLK : (b + 1) * BLK, cols(h)].astype(F32) * factor).astype(BF)
            st[p] = mm_tn(scaled, v[b * BLK : (b + 1) * BLK, cols(h)])
        t0, t1 = total_of(h), total_of(NH + h)
        whole = jnp.exp(t1) * st[h] + st[NH + h]
        for u in range(4):
            tx_s[h * 4 + u, 0:32] = whole[32 * u : 32 * u + 32]
            tx_s[h * 4 + u, 32:40] = jnp.broadcast_to(t0 + t1, (8, DK))

    def exchange(tx, rx, kind):
        copies = []
        for d in range(1, TM):
            peer = lax.rem(tm + d, TM)
            n = kind * TM + d
            copies.append(
                send(tx.at[peer], rx.at[tm], s_send.at[n], s_recv.at[n], {"tm": peer})
            )
        return copies

    s_first = exchange(tx_s, rx_s, 0)
    rx_s[tm] = tx_s[tm]
    to_across.append(gather(g_hbm, hd, 512, 512, across, 5))
    w_across = w_copy(w_hbm, tm, tm_at(1 - zl, y, core), 0)
    w_near = [
        w_copy(w_hbm, tm, tm_at(zl, lax.rem(y + d, 4), core), d) for d in range(1, 4)
    ]
    w_pair = [w_copy(w_hbm, tm, mate, 7)]

    @pl.loop(0, NH)
    def _(h):
        low = lax.broadcasted_iota(jnp.int32, (HALF, HALF), 0) >= lax.broadcasted_iota(
            jnp.int32, (HALF, HALF), 1
        )
        for b in range(2):
            p = b * NH + h
            row, urow = rows_of(p)
            at = column(row)
            grown = jnp.exp(at)
            ecol[p] = grown
            qb = q[b * BLK : (b + 1) * BLK, cols(h)]
            kb = k[b * BLK : (b + 1) * BLK, cols(h)]
            qst[p] = jnp.transpose(qb.astype(F32) * grown).astype(BF)
            wide = jnp.concatenate([at, at], axis=1)
            for n, (ti, si) in enumerate(((0, 0), (1, 0), (1, 1))):
                gap = wide[ti * HALF : (ti + 1) * HALF] - row[:, si * HALF : (si + 1) * HALF]
                if ti == si:
                    gap = jnp.where(low, gap, -jnp.inf)
                tile = jnp.exp(gap) * urow[:, si * HALF : (si + 1) * HALF]
                mask[p, n] = tile
                score = mm_nt(qb[ti * HALF : (ti + 1) * HALF], kb[si * HALF : (si + 1) * HALF])
                wts[p, n] = (tile * score).astype(BF)

    w_across.wait_recv()
    z_mate = tm_at(1 - zl, y, core)
    w_far = [
        w_copy(w_block(z_mate), z_mate, tm_at(zl, lax.rem(y + d, 4), core), 3 + d)
        for d in range(1, 4)
    ]
    w_pair.append(w_copy(w_block(z_mate), z_mate, mate, 8))
    on_right, on_left = [], []

    def pass_x(c):
        to_right[c].wait_recv()
        on_right.append(gather(grads.at[left], left, c * 512, 256, right, 6 + c))
        to_left[c].wait_recv()
        on_left.append(gather(grads.at[right], right, c * 512 + 256, 256, left, 8 + c))

    pass_x(0)

    for copy in s_first:
        copy.wait_recv()
    part = jnp.zeros((32, DK), F32)
    for i in range(TM):
        tx_p[i] = part.astype(BF)
        fall = jnp.exp(rx_s[i, 32:40])
        dec[i] = fall
        part = jnp.concatenate([fall] * 4, axis=0) * part + rx_s[i, 0:32]
    s_second = exchange(tx_p, rx_p, 1)
    rx_p[tm] = tx_p[tm]

    for d in range(1, 4):
        src = tm_at(zl, lax.rem(y + 4 - d, 4), core)
        w_near[d - 1].wait_recv()
        w_pair.append(w_copy(w_block(src), src, mate, 8 + d))
    pass_x(1)
    p_right, p_left = [], []

    def pass_z(c):
        to_across[c].wait_recv()
        p_right.append(gather(grads.at[across], across, c * 512, 512, right, 10 + c))
        p_left.append(gather(grads.at[across], across, c * 512, 512, left, 12 + c))

    pass_z(0)
    for d in range(1, 4):
        src = tm_at(1 - zl, lax.rem(y + 4 - d, 4), core)
        w_far[d - 1].wait_recv()
        w_pair.append(w_copy(w_block(src), src, mate, 11 + d))

    for copy in s_second:
        copy.wait_recv()

    @pl.loop(0, NH)
    def _(h):
        start = rx_p[pl.ds(h * 4, 4)].reshape(DK, DK).astype(F32)
        starts = (start, jnp.exp(total_of(h)) * start + st[h])
        for b in range(2):
            p = b * NH + h
            state = starts[b].astype(BF)
            sb[p] = state
            rows = slice(b * BLK, (b + 1) * BLK)
            v0 = v[b * BLK : b * BLK + HALF, cols(h)]
            v1 = v[b * BLK + HALF : (b + 1) * BLK, cols(h)]
            within = jnp.concatenate(
                [mm(wts[p, 0], v0), mm(wts[p, 1], v0) + mm(wts[p, 2], v1)], axis=0
            )
            mixed = within + ecol[p] * mm(q[rows, cols(h)], state)
            mixt[cols(h), rows] = jnp.transpose(mixed).astype(BF)

    pass_z(1)
    on_across = []

    def pass_far(c):
        on_right[c].wait_recv()
        on_across.append(gather(grads.at[far], far, c * 512, 256, across, 14 + 2 * c))
        on_left[c].wait_recv()
        on_across.append(gather(grads.at[far], far, c * 512 + 256, 256, across, 15 + 2 * c))

    pass_far(0)

    @pl.loop(0, 4)
    def _(r):
        acc[pl.ds(r * HALF, HALF), :] = jnp.zeros((HALF, NH * DK), F32)

    def grow_mixed(s):
        @pl.loop(0, 4)
        def _(r):
            rows = pl.ds(pl.multiple_of(r * HALF, HALF), HALF)
            acc[rows, :] += mm(grads[s, rows, :], weight[s])

    mine = pl.ds(pl.multiple_of(core * HALF, HALF), HALF)
    other = pl.ds(pl.multiple_of((1 - core) * HALF, HALF), HALF)
    pairs = []

    def grow_weight(s, n):
        @pl.loop(0, 2)
        def _(r):
            rows = pl.ds(pl.multiple_of(r * HALF, HALF), HALF)
            pair_tx[n, rows, :] = mm(mixt[rows, :], grads[s, :, other]).astype(BF)

        pairs.append(
            send(pair_tx.at[n], pair_rx.at[n], c_send.at[n], c_recv.at[n], {"tm": mate})
        )

        @pl.loop(0, 2)
        def _(r):
            rows = pl.ds(pl.multiple_of(r * HALF, HALF), HALF)
            pair_own[n % 4, rows, :] = mm(mixt[rows, :], grads[s, :, mine])

    def y_copy(s, n):
        gap = lax.rem(lax.rem(s, 4) + 4 - y, 4)
        slot = (s // 4) * 4
        return gap, pltpu.make_async_remote_copy(
            src_ref=y_tx.at[n],
            dst_ref=y_rx.at[slot + y],
            send_sem=y_send.at[n],
            recv_sem=y_recv.at[slot + gap],
            device_id={"tm": tm_at(zl, lax.rem(s, 4), core)},
            device_id_type=MESH,
        )

    def add_pair(s, n):
        pairs[n].wait_recv()
        y_tx[n] = (pair_own[n % 4] + pair_rx[n].astype(F32)).astype(BF)
        gap, copy = y_copy(s, n)

        @pl.when(gap != 0)
        def _():
            copy.start()

        @pl.when(gap == 0)
        def _():
            y_rx[(s // 4) * 4 + y] = y_tx[n]

    z_right = lax.rem(right + 4, 8)
    z_left = lax.rem(left + 4, 8)
    z_far = lax.rem(far + 4, 8)
    order = [hd, right, left, across, far, z_far, z_left, z_right]

    loads[3].wait()
    loads[4].wait()
    for copy in w_pair:
        copy.wait_recv()
    grow_weight(order[0], 0)
    grow_mixed(order[0])
    pass_far(1)
    for n in range(1, 4):
        grow_weight(order[n], n)
        add_pair(order[n - 1], n - 1)
        grow_mixed(order[n])
    grow_weight(order[4], 4)
    add_pair(order[3], 3)
    grow_mixed(order[4])
    for copy in on_across:
        copy.wait_recv()
    grow_weight(order[5], 5)
    add_pair(order[4], 4)
    grow_mixed(order[5])
    for copy in p_right:
        copy.wait_recv()
    grow_weight(order[6], 6)
    add_pair(order[5], 5)
    for copy in p_left:
        copy.wait_recv()
    grow_weight(order[7], 7)
    add_pair(order[6], 6)
    grow_mixed(order[6])
    add_pair(order[7], 7)
    grow_mixed(order[7])

    @pl.loop(0, 4)
    def _(r):
        rows = pl.ds(pl.multiple_of(r * HALF, HALF), HALF)
        e[rows, :] = acc[rows, :].astype(BF)

    @pl.loop(0, NH)
    def _(h):
        for b in range(2):
            rl[b * NH + h] = mm(qst[b * NH + h], e[b * BLK : (b + 1) * BLK, cols(h)])
        whole = jnp.exp(total_of(h)) * rl[NH + h] + rl[h]
        for u in range(4):
            tx_r[h * 4 + u] = whole[32 * u : 32 * u + 32].astype(BF)

    r_first = exchange(tx_r, rx_r, 2)
    rx_r[tm] = tx_r[tm]

    def local_grads(h):
        for b in range(2):
            p = b * NH + h
            rows = slice(b * BLK, (b + 1) * BLK)
            eb = e[rows, cols(h)]
            qb = q[rows, cols(h)]
            kb = k[rows, cols(h)]
            vb = v[rows, cols(h)]
            lo, hi = slice(0, HALF), slice(HALF, BLK)
            bk = []
            for n, (ti, si) in enumerate(((lo, lo), (hi, lo), (hi, hi))):
                bk.append((mask[p, n] * mm_nt(eb[ti], vb[si])).astype(BF))
            near = jnp.concatenate(
                [mm(bk[0], kb[lo]), mm(bk[1], kb[lo]) + mm(bk[2], kb[hi])], axis=0
            )
            dq_ref[rows, cols(h)] = (near + ecol[p] * mm_nt(eb, sb[p])).astype(BF)
            acc[b * BLK : b * BLK + HALF, cols(h)] = mm_tn(bk[0], qb[lo]) + mm_tn(bk[1], qb[hi])
            acc[b * BLK + HALF : (b + 1) * BLK, cols(h)] = mm_tn(bk[2], qb[hi])
            dvp[b * BLK : b * BLK + HALF, cols(h)] = mm_tn(wts[p, 0], eb[lo]) + mm_tn(
                wts[p, 1], eb[hi]
            )
            dvp[b * BLK + HALF : (b + 1) * BLK, cols(h)] = mm_tn(wts[p, 2], eb[hi])

    @pl.loop(0, 2)
    def _(h):
        local_grads(h)

    for copy in r_first:
        copy.wait_recv()
    part = jnp.zeros((32, DK), F32)
    for i in reversed(range(TM)):
        tx_o[i] = part.astype(BF)
        part = jnp.concatenate([dec[i]] * 4, axis=0) * part + rx_r[i].astype(F32)
    r_second = exchange(tx_o, rx_o, 3)
    rx_o[tm] = tx_o[tm]

    def y_arrivals(part_z):
        for d in range(1, 4):
            pltpu.make_async_remote_copy(
                src_ref=y_tx.at[0],
                dst_ref=y_rx.at[0],
                send_sem=y_send.at[0],
                recv_sem=y_recv.at[part_z * 4 + d],
                device_id={"tm": mate},
                device_id_type=MESH,
            ).wait_recv()

    def y_sum(part_z, rows):
        total = y_rx[part_z * 4, rows].astype(F32)
        for i in range(1, 4):
            total = total + y_rx[part_z * 4 + i, rows].astype(F32)
        return total

    y_arrivals(1 - zl)

    @pl.loop(0, 2)
    def _(r):
        rows = pl.ds(pl.multiple_of(r * HALF, HALF), HALF)
        z_tx[rows, :] = y_sum(1 - zl, rows).astype(BF)

    z_copy = send(z_tx, z_rx, z_send.at[0], z_recv.at[0], {"tm": z_mate})

    @pl.loop(2, NH)
    def _(h):
        local_grads(h)

    y_arrivals(zl)
    for copy in r_second:
        copy.wait_recv()

    @pl.loop(0, NH)
    def _(h):
        end = rx_o[pl.ds(h * 4, 4)].reshape(DK, DK).astype(F32)
        ends = (jnp.exp(total_of(NH + h)) * end + rl[NH + h], end)
        for b in range(2):
            p = b * NH + h
            rows = slice(b * BLK, (b + 1) * BLK)
            carried = ends[b].astype(BF)
            dk_ref[rows, cols(h)] = (
                acc[rows, cols(h)] + fcol[p] * mm_nt(v[rows, cols(h)], carried)
            ).astype(BF)
            dv_ref[rows, cols(h)] = (
                dvp[rows, cols(h)] + fcol[p] * mm(k[rows, cols(h)], carried)
            ).astype(BF)

    z_copy.wait_recv()
    for r in range(2):
        rows = slice(r * HALF, (r + 1) * HALF)
        total = y_sum(zl, rows) + z_rx[rows, :].astype(F32)
        gw_ref[:, rows] = jnp.transpose(total)

    for n in range(8):
        gap, copy = y_copy(order[n], n)

        @pl.when(gap != 0)
        def _():
            copy.wait_send()

    for copy in sent:
        copy.wait_send()


def per_device(q, k, v, g, w, periods, log_decay):
    anywhere = pl.BlockSpec(memory_space=pl.ANY)
    vmem = pl.BlockSpec(memory_space=pltpu.VMEM)
    dma = pltpu.SemaphoreType.DMA
    return pl.pallas_call(
        kernel,
        out_shape=(
            jax.ShapeDtypeStruct((ROWS, NH * DK), BF),
            jax.ShapeDtypeStruct((ROWS, NH * DK), BF),
            jax.ShapeDtypeStruct((ROWS, NH * DK), BF),
            jax.ShapeDtypeStruct((HALF, NH * DK), F32),
        ),
        in_specs=[pl.BlockSpec(memory_space=pltpu.SMEM), vmem] + [anywhere] * 5,
        out_specs=[vmem] * 4,
        scratch_shapes=[
            pltpu.VMEM((ROWS, 512), BF),
            pltpu.VMEM((ROWS, 512), BF),
            pltpu.VMEM((ROWS, 512), BF),
            pltpu.VMEM((ROWS, 512), BF),
            pltpu.VMEM((8, ROWS, 512), BF),
            pltpu.VMEM((8, 512, 512), BF),
            pltpu.VMEM((ROWS, 512), F32),
            pltpu.VMEM((8, BLK), F32),
            pltpu.VMEM((8, BLK), F32),
            pltpu.VMEM((8, BLK, DK), F32),
            pltpu.VMEM((8, BLK, DK), F32),
            pltpu.VMEM((8, 3, HALF, HALF), F32),
            pltpu.VMEM((8, 3, HALF, HALF), BF),
            pltpu.VMEM((8, DK, BLK), BF),
            pltpu.VMEM((512, ROWS), BF),
            pltpu.VMEM((8, DK, DK), F32),
            pltpu.VMEM((8, DK, DK), BF),
            pltpu.VMEM((8, DK, DK), F32),
            pltpu.VMEM((ROWS, 512), F32),
            pltpu.VMEM((TM, 40, DK), F32),
            pltpu.VMEM((TM, 40, DK), F32),
            pltpu.VMEM((TM, 32, DK), BF),
            pltpu.VMEM((TM, 32, DK), BF),
            pltpu.VMEM((TM, 32, DK), BF),
            pltpu.VMEM((TM, 32, DK), BF),
            pltpu.VMEM((TM, 32, DK), BF),
            pltpu.VMEM((TM, 32, DK), BF),
            pltpu.VMEM((TM, 8, DK), F32),
            pltpu.VMEM((8, 512, HALF), BF),
            pltpu.VMEM((8, 512, HALF), BF),
            pltpu.VMEM((4, 512, HALF), F32),
            pltpu.VMEM((8, 512, HALF), BF),
            pltpu.VMEM((8, 512, HALF), BF),
            pltpu.VMEM((512, HALF), BF),
            pltpu.VMEM((512, HALF), BF),
            dma((5,)),
            dma((18,)),
            dma((18,)),
            dma((15,)),
            dma((15,)),
            dma((64,)),
            dma((64,)),
            dma((8,)),
            dma((8,)),
            dma((8,)),
            dma((8,)),
            dma((1,)),
            dma((1,)),
        ],
        compiler_params=pltpu.CompilerParams(
            collective_id=0, has_side_effects=True, vmem_limit_bytes=66_000_000
        ),
    )(periods, log_decay, q, k, v, g, w)


def solution(mesh):
    return jax.shard_map(
        per_device,
        mesh=mesh,
        in_specs=(
            P("tm", "head"),
            P("tm", "head"),
            P("tm", "head"),
            P("tm", "head"),
            P("tm", "head"),
            P("head"),
            P("head", "tm"),
        ),
        out_specs=(P("tm", "head"), P("tm", "head"), P("tm", "head"), P("tm", "head")),
        check_vma=False,
    )
```

```python
import jax
import jax.numpy as jnp
from jax import lax
from jax.experimental import pallas as pl
from jax.experimental.pallas import tpu as pltpu
from jax.sharding import PartitionSpec as P

DK = 128
BLK = 512
NH = 4
TM = 16
ROWS = 1024
HALF = 256
BF = jnp.bfloat16
F32 = jnp.float32
MESH = pl.DeviceIdType.MESH


def mm(a, b):
    return jnp.dot(a, b, preferred_element_type=F32)


def mm_nt(a, b):
    return lax.dot_general(a, b, (((1,), (1,)), ((), ())), preferred_element_type=F32)


def mm_tn(a, b):
    return lax.dot_general(a, b, (((0,), (0,)), ((), ())), preferred_element_type=F32)


def column(row):
    return jnp.transpose(jnp.broadcast_to(row, (DK, row.shape[1])))


def kernel(
    per_ref,
    ld_ref,
    q_hbm,
    k_hbm,
    v_hbm,
    g_hbm,
    w_hbm,
    dq_ref,
    dk_ref,
    dv_ref,
    gw_ref,
    q,
    k,
    v,
    e,
    grads,
    weight,
    acc,
    cum,
    upd,
    fcol,
    ecol,
    mask,
    wts,
    qst,
    mixt,
    st,
    sb,
    rl,
    dvp,
    tx_s,
    rx_s,
    tx_p,
    rx_p,
    tx_r,
    rx_r,
    tx_o,
    rx_o,
    dec,
    pair_tx,
    pair_rx,
    pair_own,
    y_tx,
    y_rx,
    z_tx,
    z_rx,
    load_sem,
    ag_send,
    ag_recv,
    w_send,
    w_recv,
    s_send,
    s_recv,
    c_send,
    c_recv,
    y_send,
    y_recv,
    z_send,
    z_recv,
):
    tm = lax.axis_index("tm")
    hd = lax.axis_index("head")
    x = lax.rem(hd, 4)
    zh = hd // 4
    right = zh * 4 + lax.rem(x + 1, 4)
    left = zh * 4 + lax.rem(x + 3, 4)
    far = zh * 4 + lax.rem(x + 2, 4)
    across = lax.rem(hd + 4, 8)
    core = lax.rem(tm, 2)
    y = lax.rem(tm // 2, 4)
    zl = tm // 8
    mate = tm + 1 - 2 * core

    def tm_at(zl_, y_, core_):
        return (zl_ * 4 + y_) * 2 + core_

    def local(src, dst, i):
        return pltpu.make_async_copy(src, dst, load_sem.at[i])

    loads = [
        local(k_hbm, k, 0),
        local(v_hbm, v, 1),
        local(q_hbm, q, 2),
        local(g_hbm.at[:, 0:HALF], grads.at[hd, 0], 3),
        local(g_hbm.at[:, HALF:512], grads.at[hd, 1], 4),
        local(w_hbm, weight.at[tm // 2, pl.ds(core * HALF, HALF)], 5),
    ]
    for item in loads:
        item.start()

    barrier = pltpu.get_barrier_semaphore()
    for d in range(1, TM):
        pl.semaphore_signal(
            barrier, inc=1, device_id={"tm": lax.rem(tm + d, TM)}, device_id_type=MESH
        )
    for peer in (right, left, across):
        pl.semaphore_signal(barrier, inc=1, device_id={"head": peer}, device_id_type=MESH)
    pl.semaphore_wait(barrier, TM + 2)

    sent = []

    def send(src, dst, send_sem, recv_sem, device):
        copy = pltpu.make_async_remote_copy(
            src_ref=src,
            dst_ref=dst,
            send_sem=send_sem,
            recv_sem=recv_sem,
            device_id=device,
            device_id_type=MESH,
        )
        copy.start()
        sent.append(copy)
        return copy

    def gather(src, slot, c, first, count, peer, n):
        rows = pl.ds(first, count)
        if src is g_hbm:
            block = g_hbm.at[:, c * HALF : (c + 1) * HALF]
        else:
            block = grads.at[slot, c]
        return send(
            block.at[rows],
            grads.at[slot, c, rows],
            ag_send.at[n],
            ag_recv.at[n],
            {"head": peer},
        )

    to_right, to_left = [], []
    for c in range(2):
        to_right.append(gather(g_hbm, hd, c, 0, ROWS, right, c))
        to_left.append(gather(g_hbm, hd, c, 0, ROWS, left, 2 + c))

    def w_copy(src, owner, device, n):
        return send(
            src,
            weight.at[owner // 2, pl.ds(lax.rem(owner, 2) * HALF, HALF)],
            w_send.at[n],
            w_recv.at[n],
            {"tm": device},
        )

    def w_block(owner):
        return weight.at[owner // 2, pl.ds(lax.rem(owner, 2) * HALF, HALF)]

    ids = lax.broadcasted_iota(jnp.int32, (8, BLK), 0)
    lane = lax.broadcasted_iota(jnp.int32, (8, BLK), 1)
    head_of = lax.rem(ids, NH)
    period = jnp.full((8, BLK), per_ref[0], jnp.int32)
    for h in range(1, NH):
        period = jnp.where(head_of == h, per_ref[h], period)
    period = period.astype(F32)
    pos = (tm * ROWS + (ids // NH) * BLK + lane).astype(F32)
    turns = jnp.floor((pos + 0.5) * (1.0 / period))
    update = jnp.where(pos == turns * period, 1.0, 0.0).astype(F32)
    cum[0:NH, :] = ld_ref[:, 0:BLK]
    cum[NH : 2 * NH, :] = ld_ref[:, BLK : 2 * BLK]
    run = update * period * cum[...]
    shift = 1
    while shift < BLK:
        run = run + jnp.where(lane >= shift, pltpu.roll(run, shift, axis=1), 0.0)
        shift *= 2
    cum[...] = run
    upd[...] = update

    def rows_of(p):
        return cum[pl.ds(p, 1), :], upd[pl.ds(p, 1), :]

    def total_of(p):
        row = cum[pl.ds(p, 1), :]
        return jnp.broadcast_to(row[:, BLK - 1 : BLK], (1, DK))

    def cols(h):
        return pl.ds(pl.multiple_of(h * DK, DK), DK)

    loads[0].wait()
    loads[1].wait()

    @pl.loop(0, NH)
    def _(h):
        for b in range(2):
            p = b * NH + h
            row, urow = rows_of(p)
            factor = column(urow * jnp.exp(row[:, BLK - 1 : BLK] - row))
            fcol[p] = factor
            scaled = (k[b * BLK : (b + 1) * BLK, cols(h)].astype(F32) * factor).astype(BF)
            st[p] = mm_tn(scaled, v[b * BLK : (b + 1) * BLK, cols(h)])
        t0, t1 = total_of(h), total_of(NH + h)
        whole = jnp.exp(t1) * st[h] + st[NH + h]
        for u in range(4):
            tx_s[h * 4 + u, 0:32] = whole[32 * u : 32 * u + 32]
            tx_s[h * 4 + u, 32:40] = jnp.broadcast_to(t0 + t1, (8, DK))

    def exchange(tx, rx, kind):
        copies = []
        for d in range(1, TM):
            peer = lax.rem(tm + d, TM)
            n = kind * TM + d
            copies.append(
                send(tx.at[peer], rx.at[tm], s_send.at[n], s_recv.at[n], {"tm": peer})
            )
        return copies

    s_first = exchange(tx_s, rx_s, 0)
    rx_s[tm] = tx_s[tm]
    w_across = w_copy(w_hbm, tm, tm_at(1 - zl, y, core), 0)
    w_near = [
        w_copy(w_hbm, tm, tm_at(zl, lax.rem(y + d, 4), core), d) for d in range(1, 4)
    ]
    w_pair = [w_copy(w_hbm, tm, mate, 7)]
    loads[2].wait()

    @pl.loop(0, NH)
    def _(h):
        low = lax.broadcasted_iota(jnp.int32, (HALF, HALF), 0) >= lax.broadcasted_iota(
            jnp.int32, (HALF, HALF), 1
        )
        for b in range(2):
            p = b * NH + h
            row, urow = rows_of(p)
            at = column(row)
            grown = jnp.exp(at)
            ecol[p] = grown
            qb = q[b * BLK : (b + 1) * BLK, cols(h)]
            kb = k[b * BLK : (b + 1) * BLK, cols(h)]
            qst[p] = jnp.transpose(qb.astype(F32) * grown).astype(BF)
            wide = jnp.concatenate([at, at], axis=1)
            for n, (ti, si) in enumerate(((0, 0), (1, 0), (1, 1))):
                gap = wide[ti * HALF : (ti + 1) * HALF] - row[:, si * HALF : (si + 1) * HALF]
                if ti == si:
                    gap = jnp.where(low, gap, -jnp.inf)
                tile = jnp.exp(gap) * urow[:, si * HALF : (si + 1) * HALF]
                mask[p, n] = tile
                score = mm_nt(qb[ti * HALF : (ti + 1) * HALF], kb[si * HALF : (si + 1) * HALF])
                wts[p, n] = (tile * score).astype(BF)

    for copy in s_first:
        copy.wait_recv()
    part = jnp.zeros((32, DK), F32)
    for i in range(TM):
        tx_p[i] = part.astype(BF)
        fall = jnp.exp(rx_s[i, 32:40])
        dec[i] = fall
        part = jnp.concatenate([fall] * 4, axis=0) * part + rx_s[i, 0:32]
    s_second = exchange(tx_p, rx_p, 1)
    rx_p[tm] = tx_p[tm]
    to_across = [gather(g_hbm, hd, c, 0, ROWS, across, 4 + c) for c in range(2)]

    w_across.wait_recv()
    z_mate = tm_at(1 - zl, y, core)
    w_far = [
        w_copy(w_block(z_mate), z_mate, tm_at(zl, lax.rem(y + d, 4), core), 3 + d)
        for d in range(1, 4)
    ]
    w_pair.append(w_copy(w_block(z_mate), z_mate, mate, 8))
    on_right, on_left = [], []

    def pass_x(c):
        to_right[c].wait_recv()
        on_right.append(gather(grads, left, c, 0, 512, right, 6 + c))
        to_left[c].wait_recv()
        on_left.append(gather(grads, right, c, 512, 512, left, 8 + c))

    p_right, p_left = [], []

    def pass_z(c):
        to_across[c].wait_recv()
        p_right.append(gather(grads, across, c, 0, ROWS, right, 10 + c))
        p_left.append(gather(grads, across, c, 0, ROWS, left, 12 + c))

    on_across = []

    def pass_far(c):
        on_right[c].wait_recv()
        on_across.append(gather(grads, far, c, 0, 512, across, 14 + 2 * c))
        on_left[c].wait_recv()
        on_across.append(gather(grads, far, c, 512, 512, across, 15 + 2 * c))

    pass_x(0)

    for copy in s_second:
        copy.wait_recv()

    @pl.loop(0, NH)
    def _(h):
        start = rx_p[pl.ds(h * 4, 4)].reshape(DK, DK).astype(F32)
        starts = (start, jnp.exp(total_of(h)) * start + st[h])
        for b in range(2):
            p = b * NH + h
            state = starts[b].astype(BF)
            sb[p] = state
            rows = slice(b * BLK, (b + 1) * BLK)
            v0 = v[b * BLK : b * BLK + HALF, cols(h)]
            v1 = v[b * BLK + HALF : (b + 1) * BLK, cols(h)]
            within = jnp.concatenate(
                [mm(wts[p, 0], v0), mm(wts[p, 1], v0) + mm(wts[p, 2], v1)], axis=0
            )
            mixed = within + ecol[p] * mm(q[rows, cols(h)], state)
            mixt[cols(h), rows] = jnp.transpose(mixed).astype(BF)

    @pl.loop(0, 4)
    def _(r):
        acc[pl.ds(r * HALF, HALF), :] = jnp.zeros((HALF, NH * DK), F32)

    def w_rows(s, c):
        return weight[s, c * HALF : (c + 1) * HALF, :]

    def grow_mixed(*units):
        @pl.loop(0, 4)
        def _(r):
            rows = pl.ds(pl.multiple_of(r * HALF, HALF), HALF)
            total = acc[rows, :]
            for s, c in units:
                total = total + mm(grads[s, c, rows, :], w_rows(s, c))
            acc[rows, :] = total

    mine = pl.ds(pl.multiple_of(core * HALF, HALF), HALF)
    other = pl.ds(pl.multiple_of((1 - core) * HALF, HALF), HALF)
    units = []
    pairs = []
    y_sent = []

    def grow_weight(s, c):
        n = len(units)
        units.append((s, c))
        pair_tx[n] = mm(mixt[other, :], grads[s, c]).astype(BF)
        pairs.append(
            send(pair_tx.at[n], pair_rx.at[n], c_send.at[n], c_recv.at[n], {"tm": mate})
        )
        pair_own[n % 8] = mm(mixt[mine, :], grads[s, c])

    def add_pairs():
        for n in range(len(y_sent), len(units)):
            s, c = units[n]
            pairs[n].wait_recv()
            y_tx[n] = (pair_own[n % 8] + pair_rx[n].astype(F32)).astype(BF)
            gap = lax.rem(lax.rem(s, 4) + 4 - y, 4)
            part_z = s // 4
            copy = pltpu.make_async_remote_copy(
                src_ref=y_tx.at[n],
                dst_ref=y_rx.at[part_z, y, core],
                send_sem=y_send.at[n],
                recv_sem=y_recv.at[part_z, gap, core],
                device_id={"tm": tm_at(zl, lax.rem(s, 4), c)},
                device_id_type=MESH,
            )
            away = jnp.logical_or(gap != 0, core != c)

            @pl.when(away)
            def _():
                copy.start()

            @pl.when(jnp.logical_not(away))
            def _():
                y_rx[part_z, y, core] = y_tx[n]

            y_sent.append((away, copy))

    z_right = lax.rem(right + 4, 8)
    z_left = lax.rem(left + 4, 8)
    z_far = lax.rem(far + 4, 8)

    loads[3].wait()
    loads[4].wait()
    grow_weight(hd, 0)
    grow_weight(hd, 1)
    pass_x(1)
    pass_z(0)
    add_pairs()
    for c in range(2):
        grow_weight(left, c)
        grow_weight(right, c)
    for d in range(1, 4):
        src = tm_at(zl, lax.rem(y + 4 - d, 4), core)
        w_near[d - 1].wait_recv()
        w_pair.append(w_copy(w_block(src), src, mate, 8 + d))
    add_pairs()
    pass_far(0)
    grow_weight(across, 0)
    grow_weight(far, 0)
    pass_z(1)
    add_pairs()
    grow_weight(across, 1)
    for d in range(1, 4):
        src = tm_at(1 - zl, lax.rem(y + 4 - d, 4), core)
        w_far[d - 1].wait_recv()
        w_pair.append(w_copy(w_block(src), src, mate, 11 + d))
    pass_far(1)
    grow_weight(far, 1)
    add_pairs()
    loads[5].wait()
    for copy in w_pair:
        copy.wait_recv()
    grow_mixed(*units[0:5])
    grow_mixed(*units[5:10])
    for copy in (p_right[0], p_left[0], on_across[0], on_across[1]):
        copy.wait_recv()
    grow_weight(z_left, 0)
    grow_weight(z_right, 0)
    grow_weight(z_far, 0)
    grow_mixed(*units[10:13])
    add_pairs()
    for copy in (on_across[2], on_across[3]):
        copy.wait_recv()
    grow_weight(z_far, 1)
    grow_mixed(units[13])
    add_pairs()
    p_right[1].wait_recv()
    p_left[1].wait_recv()
    grow_weight(z_left, 1)
    grow_weight(z_right, 1)
    grow_mixed(*units[14:16])
    add_pairs()

    @pl.loop(0, 4)
    def _(r):
        rows = pl.ds(pl.multiple_of(r * HALF, HALF), HALF)
        e[rows, :] = acc[rows, :].astype(BF)

    @pl.loop(0, NH)
    def _(h):
        for b in range(2):
            rl[b * NH + h] = mm(qst[b * NH + h], e[b * BLK : (b + 1) * BLK, cols(h)])
        whole = jnp.exp(total_of(h)) * rl[NH + h] + rl[h]
        for u in range(4):
            tx_r[h * 4 + u] = whole[32 * u : 32 * u + 32].astype(BF)

    r_first = exchange(tx_r, rx_r, 2)
    rx_r[tm] = tx_r[tm]

    def local_grads(h):
        for b in range(2):
            p = b * NH + h
            rows = slice(b * BLK, (b + 1) * BLK)
            eb = e[rows, cols(h)]
            qb = q[rows, cols(h)]
            kb = k[rows, cols(h)]
            vb = v[rows, cols(h)]
            lo, hi = slice(0, HALF), slice(HALF, BLK)
            bk = []
            for n, (ti, si) in enumerate(((lo, lo), (hi, lo), (hi, hi))):
                bk.append((mask[p, n] * mm_nt(eb[ti], vb[si])).astype(BF))
            near = jnp.concatenate(
                [mm(bk[0], kb[lo]), mm(bk[1], kb[lo]) + mm(bk[2], kb[hi])], axis=0
            )
            dq_ref[rows, cols(h)] = (near + ecol[p] * mm_nt(eb, sb[p])).astype(BF)
            acc[b * BLK : b * BLK + HALF, cols(h)] = mm_tn(bk[0], qb[lo]) + mm_tn(bk[1], qb[hi])
            acc[b * BLK + HALF : (b + 1) * BLK, cols(h)] = mm_tn(bk[2], qb[hi])
            dvp[b * BLK : b * BLK + HALF, cols(h)] = mm_tn(wts[p, 0], eb[lo]) + mm_tn(
                wts[p, 1], eb[hi]
            )
            dvp[b * BLK + HALF : (b + 1) * BLK, cols(h)] = mm_tn(wts[p, 2], eb[hi])

    @pl.loop(0, 2)
    def _(h):
        local_grads(h)

    for copy in r_first:
        copy.wait_recv()
    part = jnp.zeros((32, DK), F32)
    for i in reversed(range(TM)):
        tx_o[i] = part.astype(BF)
        part = jnp.concatenate([dec[i]] * 4, axis=0) * part + rx_r[i].astype(F32)
    r_second = exchange(tx_o, rx_o, 3)
    rx_o[tm] = tx_o[tm]

    def y_arrivals(part_z):
        def arrive(gap, half):
            pltpu.make_async_remote_copy(
                src_ref=y_tx.at[0],
                dst_ref=y_rx.at[0, 0, 0],
                send_sem=y_send.at[0],
                recv_sem=y_recv.at[part_z, gap, half],
                device_id={"tm": mate},
                device_id_type=MESH,
            ).wait_recv()

        for gap in range(1, 4):
            for half in range(2):
                arrive(gap, half)
        arrive(0, 1 - core)

    def y_sum(part_z, half):
        total = y_rx[part_z, 0, half].astype(F32)
        for i in range(1, 4):
            total = total + y_rx[part_z, i, half].astype(F32)
        return total

    y_arrivals(1 - zl)

    for r in range(2):
        z_tx[r * HALF : (r + 1) * HALF, :] = y_sum(1 - zl, r).astype(BF)

    z_copy = send(z_tx, z_rx, z_send.at[0], z_recv.at[0], {"tm": z_mate})

    @pl.loop(2, NH)
    def _(h):
        local_grads(h)

    y_arrivals(zl)
    for copy in r_second:
        copy.wait_recv()

    @pl.loop(0, NH)
    def _(h):
        end = rx_o[pl.ds(h * 4, 4)].reshape(DK, DK).astype(F32)
        ends = (jnp.exp(total_of(NH + h)) * end + rl[NH + h], end)
        for b in range(2):
            p = b * NH + h
            rows = slice(b * BLK, (b + 1) * BLK)
            carried = ends[b].astype(BF)
            dk_ref[rows, cols(h)] = (
                acc[rows, cols(h)] + fcol[p] * mm_nt(v[rows, cols(h)], carried)
            ).astype(BF)
            dv_ref[rows, cols(h)] = (
                dvp[rows, cols(h)] + fcol[p] * mm(k[rows, cols(h)], carried)
            ).astype(BF)

    z_copy.wait_recv()
    for r in range(2):
        rows = slice(r * HALF, (r + 1) * HALF)
        total = y_sum(zl, r) + z_rx[rows, :].astype(F32)
        gw_ref[:, rows] = jnp.transpose(total)

    for away, copy in y_sent:

        @pl.when(away)
        def _():
            copy.wait_send()

    for copy in sent:
        copy.wait_send()


def per_device(q, k, v, g, w, periods, log_decay):
    anywhere = pl.BlockSpec(memory_space=pl.ANY)
    vmem = pl.BlockSpec(memory_space=pltpu.VMEM)
    dma = pltpu.SemaphoreType.DMA
    return pl.pallas_call(
        kernel,
        out_shape=(
            jax.ShapeDtypeStruct((ROWS, NH * DK), BF),
            jax.ShapeDtypeStruct((ROWS, NH * DK), BF),
            jax.ShapeDtypeStruct((ROWS, NH * DK), BF),
            jax.ShapeDtypeStruct((HALF, NH * DK), F32),
        ),
        in_specs=[pl.BlockSpec(memory_space=pltpu.SMEM), vmem] + [anywhere] * 5,
        out_specs=[vmem] * 4,
        scratch_shapes=[
            pltpu.VMEM((ROWS, 512), BF),
            pltpu.VMEM((ROWS, 512), BF),
            pltpu.VMEM((ROWS, 512), BF),
            pltpu.VMEM((ROWS, 512), BF),
            pltpu.VMEM((8, 2, ROWS, HALF), BF),
            pltpu.VMEM((8, 512, 512), BF),
            pltpu.VMEM((ROWS, 512), F32),
            pltpu.VMEM((8, BLK), F32),
            pltpu.VMEM((8, BLK), F32),
            pltpu.VMEM((8, BLK, DK), F32),
            pltpu.VMEM((8, BLK, DK), F32),
            pltpu.VMEM((8, 3, HALF, HALF), F32),
            pltpu.VMEM((8, 3, HALF, HALF), BF),
            pltpu.VMEM((8, DK, BLK), BF),
            pltpu.VMEM((512, ROWS), BF),
            pltpu.VMEM((8, DK, DK), F32),
            pltpu.VMEM((8, DK, DK), BF),
            pltpu.VMEM((8, DK, DK), F32),
            pltpu.VMEM((ROWS, 512), F32),
            pltpu.VMEM((TM, 40, DK), F32),
            pltpu.VMEM((TM, 40, DK), F32),
            pltpu.VMEM((TM, 32, DK), BF),
            pltpu.VMEM((TM, 32, DK), BF),
            pltpu.VMEM((TM, 32, DK), BF),
            pltpu.VMEM((TM, 32, DK), BF),
            pltpu.VMEM((TM, 32, DK), BF),
            pltpu.VMEM((TM, 32, DK), BF),
            pltpu.VMEM((TM, 8, DK), F32),
            pltpu.VMEM((16, HALF, HALF), BF),
            pltpu.VMEM((16, HALF, HALF), BF),
            pltpu.VMEM((8, HALF, HALF), F32),
            pltpu.VMEM((16, HALF, HALF), BF),
            pltpu.VMEM((2, 4, 2, HALF, HALF), BF),
            pltpu.VMEM((512, HALF), BF),
            pltpu.VMEM((512, HALF), BF),
            dma((6,)),
            dma((18,)),
            dma((18,)),
            dma((15,)),
            dma((15,)),
            dma((64,)),
            dma((64,)),
            dma((16,)),
            dma((16,)),
            dma((16,)),
            dma((2, 4, 2)),
            dma((1,)),
            dma((1,)),
        ],
        compiler_params=pltpu.CompilerParams(
            collective_id=0, has_side_effects=True, vmem_limit_bytes=66_000_000
        ),
    )(periods, log_decay, q, k, v, g, w)


def solution(mesh):
    return jax.shard_map(
        per_device,
        mesh=mesh,
        in_specs=(
            P("tm", "head"),
            P("tm", "head"),
            P("tm", "head"),
            P("tm", "head"),
            P("tm", "head"),
            P("head"),
            P("head", "tm"),
        ),
        out_specs=(P("tm", "head"), P("tm", "head"), P("tm", "head"), P("tm", "head")),
        check_vma=False,
    )
```

```python
import jax
import jax.numpy as jnp
from jax import lax
from jax.experimental import pallas as pl
from jax.experimental.pallas import tpu as pltpu
from jax.sharding import PartitionSpec as P

DK = 128
BLK = 512
NH = 4
TM = 16
ROWS = 1024
HALF = 256
BF = jnp.bfloat16
F32 = jnp.float32
MESH = pl.DeviceIdType.MESH


def mm(a, b):
    return jnp.dot(a, b, preferred_element_type=F32)


def mm_nt(a, b):
    return lax.dot_general(a, b, (((1,), (1,)), ((), ())), preferred_element_type=F32)


def mm_tn(a, b):
    return lax.dot_general(a, b, (((0,), (0,)), ((), ())), preferred_element_type=F32)


def column(row):
    return jnp.transpose(jnp.broadcast_to(row, (DK, row.shape[1])))


def kernel(
    per_ref,
    ld_ref,
    q_hbm,
    k_hbm,
    v_hbm,
    g_hbm,
    w_hbm,
    dq_ref,
    dk_ref,
    dv_ref,
    gw_ref,
    q,
    k,
    v,
    e,
    grads,
    weight,
    acc,
    cum,
    upd,
    fcol,
    ecol,
    mask,
    wts,
    qst,
    mixt,
    st,
    sb,
    rl,
    dvp,
    tx_s,
    rx_s,
    tx_p,
    rx_p,
    tx_r,
    rx_r,
    tx_o,
    rx_o,
    dec,
    pair_tx,
    pair_rx,
    pair_own,
    y_tx,
    y_rx,
    z_tx,
    z_rx,
    load_sem,
    ag_send,
    ag_recv,
    w_send,
    w_recv,
    s_send,
    s_recv,
    c_send,
    c_recv,
    y_send,
    y_recv,
    z_send,
    z_recv,
):
    tm = lax.axis_index("tm")
    hd = lax.axis_index("head")
    x = lax.rem(hd, 4)
    zh = hd // 4
    right = zh * 4 + lax.rem(x + 1, 4)
    left = zh * 4 + lax.rem(x + 3, 4)
    far = zh * 4 + lax.rem(x + 2, 4)
    across = lax.rem(hd + 4, 8)
    core = lax.rem(tm, 2)
    y = lax.rem(tm // 2, 4)
    zl = tm // 8
    mate = tm + 1 - 2 * core

    def tm_at(zl_, y_, core_):
        return (zl_ * 4 + y_) * 2 + core_

    def local(src, dst, i):
        return pltpu.make_async_copy(src, dst, load_sem.at[i])

    loads = [
        local(k_hbm, k, 0),
        local(v_hbm, v, 1),
        local(q_hbm, q, 2),
        local(g_hbm.at[:, 0:HALF], grads.at[hd, 0], 3),
        local(g_hbm.at[:, HALF:512], grads.at[hd, 1], 4),
        local(w_hbm, weight.at[tm // 2, pl.ds(core * HALF, HALF)], 5),
    ]
    for item in loads:
        item.start()

    barrier = pltpu.get_barrier_semaphore()
    for d in range(1, TM):
        pl.semaphore_signal(
            barrier, inc=1, device_id={"tm": lax.rem(tm + d, TM)}, device_id_type=MESH
        )
    for peer in (right, left, across):
        pl.semaphore_signal(barrier, inc=1, device_id={"head": peer}, device_id_type=MESH)
    ids = lax.broadcasted_iota(jnp.int32, (8, BLK), 0)
    lane = lax.broadcasted_iota(jnp.int32, (8, BLK), 1)
    head_of = lax.rem(ids, NH)
    period = jnp.full((8, BLK), per_ref[0], jnp.int32)
    for h in range(1, NH):
        period = jnp.where(head_of == h, per_ref[h], period)
    period = period.astype(F32)
    pos = (tm * ROWS + (ids // NH) * BLK + lane).astype(F32)
    turns = jnp.floor((pos + 0.5) * (1.0 / period))
    update = jnp.where(pos == turns * period, 1.0, 0.0).astype(F32)
    cum[0:NH, :] = ld_ref[:, 0:BLK]
    cum[NH : 2 * NH, :] = ld_ref[:, BLK : 2 * BLK]
    run = update * period * cum[...]
    shift = 1
    while shift < BLK:
        run = run + jnp.where(lane >= shift, pltpu.roll(run, shift, axis=1), 0.0)
        shift *= 2
    cum[...] = run
    upd[...] = update

    pl.semaphore_wait(barrier, TM + 2)

    sent = []

    def send(src, dst, send_sem, recv_sem, device):
        copy = pltpu.make_async_remote_copy(
            src_ref=src,
            dst_ref=dst,
            send_sem=send_sem,
            recv_sem=recv_sem,
            device_id=device,
            device_id_type=MESH,
        )
        copy.start()
        sent.append(copy)
        return copy

    def gather(src, slot, c, first, count, peer, n):
        rows = pl.ds(first, count)
        if src is g_hbm:
            block = g_hbm.at[:, c * HALF : (c + 1) * HALF]
        else:
            block = grads.at[slot, c]
        return send(
            block.at[rows],
            grads.at[slot, c, rows],
            ag_send.at[n],
            ag_recv.at[n],
            {"head": peer},
        )

    to_right, to_left = [], []
    for c in range(2):
        to_right.append(gather(g_hbm, hd, c, 0, ROWS, right, c))
        to_left.append(gather(g_hbm, hd, c, 0, ROWS, left, 2 + c))
    to_across = [gather(g_hbm, hd, 0, 0, ROWS, across, 4)]

    def w_copy(src, owner, device, n):
        return send(
            src,
            weight.at[owner // 2, pl.ds(lax.rem(owner, 2) * HALF, HALF)],
            w_send.at[n],
            w_recv.at[n],
            {"tm": device},
        )

    def w_block(owner):
        return weight.at[owner // 2, pl.ds(lax.rem(owner, 2) * HALF, HALF)]

    def rows_of(p):
        return cum[pl.ds(p, 1), :], upd[pl.ds(p, 1), :]

    def total_of(p):
        row = cum[pl.ds(p, 1), :]
        return jnp.broadcast_to(row[:, BLK - 1 : BLK], (1, DK))

    def cols(h):
        return pl.ds(pl.multiple_of(h * DK, DK), DK)

    loads[0].wait()
    loads[1].wait()

    @pl.loop(0, NH)
    def _(h):
        for b in range(2):
            p = b * NH + h
            row, urow = rows_of(p)
            factor = column(urow * jnp.exp(row[:, BLK - 1 : BLK] - row))
            fcol[p] = factor
            scaled = (k[b * BLK : (b + 1) * BLK, cols(h)].astype(F32) * factor).astype(BF)
            st[p] = mm_tn(scaled, v[b * BLK : (b + 1) * BLK, cols(h)])
        t0, t1 = total_of(h), total_of(NH + h)
        whole = jnp.exp(t1) * st[h] + st[NH + h]
        for u in range(4):
            tx_s[h * 4 + u, 0:32] = whole[32 * u : 32 * u + 32]
            tx_s[h * 4 + u, 32:40] = jnp.broadcast_to(t0 + t1, (8, DK))

    def exchange(tx, rx, kind):
        copies = []
        for d in range(1, TM):
            peer = lax.rem(tm + d, TM)
            n = kind * TM + d
            copies.append(
                send(tx.at[peer], rx.at[tm], s_send.at[n], s_recv.at[n], {"tm": peer})
            )
        return copies

    s_first = exchange(tx_s, rx_s, 0)
    rx_s[tm] = tx_s[tm]
    w_across = w_copy(w_hbm, tm, tm_at(1 - zl, y, core), 0)
    w_near = [
        w_copy(w_hbm, tm, tm_at(zl, lax.rem(y + d, 4), core), d) for d in range(1, 4)
    ]
    w_pair = [w_copy(w_hbm, tm, mate, 7)]
    loads[2].wait()

    @pl.loop(0, NH)
    def _(h):
        low = lax.broadcasted_iota(jnp.int32, (HALF, HALF), 0) >= lax.broadcasted_iota(
            jnp.int32, (HALF, HALF), 1
        )
        for b in range(2):
            p = b * NH + h
            row, urow = rows_of(p)
            at = column(row)
            grown = jnp.exp(at)
            ecol[p] = grown
            qb = q[b * BLK : (b + 1) * BLK, cols(h)]
            kb = k[b * BLK : (b + 1) * BLK, cols(h)]
            qst[p] = jnp.transpose(qb.astype(F32) * grown).astype(BF)
            wide = jnp.concatenate([at, at], axis=1)
            for n, (ti, si) in enumerate(((0, 0), (1, 0), (1, 1))):
                gap = wide[ti * HALF : (ti + 1) * HALF] - row[:, si * HALF : (si + 1) * HALF]
                if ti == si:
                    gap = jnp.where(low, gap, -jnp.inf)
                tile = jnp.exp(gap) * urow[:, si * HALF : (si + 1) * HALF]
                mask[p, n] = tile
                score = mm_nt(qb[ti * HALF : (ti + 1) * HALF], kb[si * HALF : (si + 1) * HALF])
                wts[p, n] = (tile * score).astype(BF)

    for copy in s_first:
        copy.wait_recv()
    part = jnp.zeros((32, DK), F32)
    for i in range(TM):
        tx_p[i] = part.astype(BF)
        fall = jnp.exp(rx_s[i, 32:40])
        dec[i] = fall
        part = jnp.concatenate([fall] * 4, axis=0) * part + rx_s[i, 0:32]
    s_second = exchange(tx_p, rx_p, 1)
    rx_p[tm] = tx_p[tm]
    to_across.append(gather(g_hbm, hd, 1, 0, ROWS, across, 5))

    on_right, on_left = [], []

    def pass_x(c):
        to_right[c].wait_recv()
        on_right.append(gather(grads, left, c, 0, 512, right, 6 + c))
        to_left[c].wait_recv()
        on_left.append(gather(grads, right, c, 512, 512, left, 8 + c))

    p_right, p_left = [], []

    def pass_z(c):
        to_across[c].wait_recv()
        p_right.append(gather(grads, across, c, 0, ROWS, right, 10 + c))
        p_left.append(gather(grads, across, c, 0, ROWS, left, 12 + c))

    on_across = []

    def pass_far(c):
        on_right[c].wait_recv()
        on_across.append(gather(grads, far, c, 0, 512, across, 14 + 2 * c))
        on_left[c].wait_recv()
        on_across.append(gather(grads, far, c, 512, 512, across, 15 + 2 * c))

    pass_x(0)
    w_across.wait_recv()
    z_mate = tm_at(1 - zl, y, core)
    w_far = [
        w_copy(w_block(z_mate), z_mate, tm_at(zl, lax.rem(y + d, 4), core), 3 + d)
        for d in range(1, 4)
    ]
    w_pair.append(w_copy(w_block(z_mate), z_mate, mate, 8))

    for copy in s_second:
        copy.wait_recv()

    @pl.loop(0, NH)
    def _(h):
        start = rx_p[pl.ds(h * 4, 4)].reshape(DK, DK).astype(F32)
        starts = (start, jnp.exp(total_of(h)) * start + st[h])
        for b in range(2):
            p = b * NH + h
            state = starts[b].astype(BF)
            sb[p] = state
            rows = slice(b * BLK, (b + 1) * BLK)
            v0 = v[b * BLK : b * BLK + HALF, cols(h)]
            v1 = v[b * BLK + HALF : (b + 1) * BLK, cols(h)]
            within = jnp.concatenate(
                [mm(wts[p, 0], v0), mm(wts[p, 1], v0) + mm(wts[p, 2], v1)], axis=0
            )
            mixed = within + ecol[p] * mm(q[rows, cols(h)], state)
            mixt[cols(h), rows] = jnp.transpose(mixed).astype(BF)

    @pl.loop(0, 4)
    def _(r):
        acc[pl.ds(r * HALF, HALF), :] = jnp.zeros((HALF, NH * DK), F32)

    def w_rows(s, c):
        return weight[s, c * HALF : (c + 1) * HALF, :]

    def grow_mixed(*units):
        @pl.loop(0, 4)
        def _(r):
            rows = pl.ds(pl.multiple_of(r * HALF, HALF), HALF)
            total = acc[rows, :]
            for s, c in units:
                total = total + mm(grads[s, c, rows, :], w_rows(s, c))
            acc[rows, :] = total

    mine = pl.ds(pl.multiple_of(core * HALF, HALF), HALF)
    other = pl.ds(pl.multiple_of((1 - core) * HALF, HALF), HALF)
    units = []
    pairs = []
    y_sent = []

    def grow_weight(s, c):
        n = len(units)
        units.append((s, c))
        pair_tx[n] = mm(mixt[other, :], grads[s, c]).astype(BF)
        pairs.append(
            send(pair_tx.at[n], pair_rx.at[n], c_send.at[n], c_recv.at[n], {"tm": mate})
        )
        pair_own[n % 8] = mm(mixt[mine, :], grads[s, c])

    def add_pairs():
        for n in range(len(y_sent), len(units)):
            s, c = units[n]
            pairs[n].wait_recv()
            y_tx[n] = (pair_own[n % 8] + pair_rx[n].astype(F32)).astype(BF)
            gap = lax.rem(lax.rem(s, 4) + 4 - y, 4)
            part_z = s // 4
            copy = pltpu.make_async_remote_copy(
                src_ref=y_tx.at[n],
                dst_ref=y_rx.at[part_z, y, core],
                send_sem=y_send.at[n],
                recv_sem=y_recv.at[part_z, gap, core],
                device_id={"tm": tm_at(zl, lax.rem(s, 4), c)},
                device_id_type=MESH,
            )
            away = jnp.logical_or(gap != 0, core != c)

            @pl.when(away)
            def _():
                copy.start()

            @pl.when(jnp.logical_not(away))
            def _():
                y_rx[part_z, y, core] = y_tx[n]

            y_sent.append((away, copy))

    z_right = lax.rem(right + 4, 8)
    z_left = lax.rem(left + 4, 8)
    z_far = lax.rem(far + 4, 8)

    loads[3].wait()
    loads[4].wait()
    grow_weight(hd, 0)
    grow_weight(hd, 1)
    pass_x(1)
    pass_z(0)
    add_pairs()
    for c in range(2):
        grow_weight(left, c)
        grow_weight(right, c)
    for d in range(1, 4):
        src = tm_at(zl, lax.rem(y + 4 - d, 4), core)
        w_near[d - 1].wait_recv()
        w_pair.append(w_copy(w_block(src), src, mate, 8 + d))
    add_pairs()
    pass_far(0)
    grow_weight(across, 0)
    grow_weight(far, 0)
    pass_z(1)
    add_pairs()
    grow_weight(across, 1)
    for d in range(1, 4):
        src = tm_at(1 - zl, lax.rem(y + 4 - d, 4), core)
        w_far[d - 1].wait_recv()
        w_pair.append(w_copy(w_block(src), src, mate, 11 + d))
    pass_far(1)
    grow_weight(far, 1)
    add_pairs()
    loads[5].wait()
    for copy in w_pair:
        copy.wait_recv()
    grow_mixed(*units[0:5])
    grow_mixed(*units[5:10])
    for copy in (p_right[0], p_left[0], on_across[0], on_across[1]):
        copy.wait_recv()
    grow_weight(z_left, 0)
    grow_weight(z_right, 0)
    grow_weight(z_far, 0)
    grow_mixed(*units[10:13])
    add_pairs()
    for copy in (on_across[2], on_across[3]):
        copy.wait_recv()
    grow_weight(z_far, 1)
    grow_mixed(units[13])
    add_pairs()
    p_right[1].wait_recv()
    p_left[1].wait_recv()
    grow_mixed((z_left, 1), (z_right, 1))

    @pl.loop(0, 4)
    def _(r):
        rows = pl.ds(pl.multiple_of(r * HALF, HALF), HALF)
        e[rows, :] = acc[rows, :].astype(BF)

    @pl.loop(0, NH)
    def _(h):
        for b in range(2):
            rl[b * NH + h] = mm(qst[b * NH + h], e[b * BLK : (b + 1) * BLK, cols(h)])
        whole = jnp.exp(total_of(h)) * rl[NH + h] + rl[h]
        for u in range(4):
            tx_r[h * 4 + u] = whole[32 * u : 32 * u + 32].astype(BF)

    r_first = exchange(tx_r, rx_r, 2)
    rx_r[tm] = tx_r[tm]
    grow_weight(z_left, 1)
    grow_weight(z_right, 1)
    add_pairs()

    def local_grads(h):
        for b in range(2):
            p = b * NH + h
            rows = slice(b * BLK, (b + 1) * BLK)
            eb = e[rows, cols(h)]
            qb = q[rows, cols(h)]
            kb = k[rows, cols(h)]
            vb = v[rows, cols(h)]
            lo, hi = slice(0, HALF), slice(HALF, BLK)
            bk = []
            for n, (ti, si) in enumerate(((lo, lo), (hi, lo), (hi, hi))):
                bk.append((mask[p, n] * mm_nt(eb[ti], vb[si])).astype(BF))
            near = jnp.concatenate(
                [mm(bk[0], kb[lo]), mm(bk[1], kb[lo]) + mm(bk[2], kb[hi])], axis=0
            )
            dq_ref[rows, cols(h)] = (near + ecol[p] * mm_nt(eb, sb[p])).astype(BF)
            acc[b * BLK : b * BLK + HALF, cols(h)] = mm_tn(bk[0], qb[lo]) + mm_tn(bk[1], qb[hi])
            acc[b * BLK + HALF : (b + 1) * BLK, cols(h)] = mm_tn(bk[2], qb[hi])
            dvp[b * BLK : b * BLK + HALF, cols(h)] = mm_tn(wts[p, 0], eb[lo]) + mm_tn(
                wts[p, 1], eb[hi]
            )
            dvp[b * BLK + HALF : (b + 1) * BLK, cols(h)] = mm_tn(wts[p, 2], eb[hi])

    @pl.loop(0, 2)
    def _(h):
        local_grads(h)

    for copy in r_first:
        copy.wait_recv()
    part = jnp.zeros((32, DK), F32)
    for i in reversed(range(TM)):
        tx_o[i] = part.astype(BF)
        part = jnp.concatenate([dec[i]] * 4, axis=0) * part + rx_r[i].astype(F32)
    r_second = exchange(tx_o, rx_o, 3)
    rx_o[tm] = tx_o[tm]

    def y_arrivals(part_z):
        def arrive(gap, half):
            pltpu.make_async_remote_copy(
                src_ref=y_tx.at[0],
                dst_ref=y_rx.at[0, 0, 0],
                send_sem=y_send.at[0],
                recv_sem=y_recv.at[part_z, gap, half],
                device_id={"tm": mate},
                device_id_type=MESH,
            ).wait_recv()

        for gap in range(1, 4):
            for half in range(2):
                arrive(gap, half)
        arrive(0, 1 - core)

    def y_sum(part_z, half):
        total = y_rx[part_z, 0, half].astype(F32)
        for i in range(1, 4):
            total = total + y_rx[part_z, i, half].astype(F32)
        return total

    y_arrivals(1 - zl)

    for r in range(2):
        z_tx[r * HALF : (r + 1) * HALF, :] = y_sum(1 - zl, r).astype(BF)

    z_copy = send(z_tx, z_rx, z_send.at[0], z_recv.at[0], {"tm": z_mate})

    @pl.loop(2, NH)
    def _(h):
        local_grads(h)

    y_arrivals(zl)
    for copy in r_second:
        copy.wait_recv()

    @pl.loop(0, NH)
    def _(h):
        end = rx_o[pl.ds(h * 4, 4)].reshape(DK, DK).astype(F32)
        ends = (jnp.exp(total_of(NH + h)) * end + rl[NH + h], end)
        for b in range(2):
            p = b * NH + h
            rows = slice(b * BLK, (b + 1) * BLK)
            carried = ends[b].astype(BF)
            dk_ref[rows, cols(h)] = (
                acc[rows, cols(h)] + fcol[p] * mm_nt(v[rows, cols(h)], carried)
            ).astype(BF)
            dv_ref[rows, cols(h)] = (
                dvp[rows, cols(h)] + fcol[p] * mm(k[rows, cols(h)], carried)
            ).astype(BF)

    z_copy.wait_recv()
    for r in range(2):
        rows = slice(r * HALF, (r + 1) * HALF)
        total = y_sum(zl, r) + z_rx[rows, :].astype(F32)
        gw_ref[:, rows] = jnp.transpose(total)

    for away, copy in y_sent:

        @pl.when(away)
        def _():
            copy.wait_send()

    for copy in sent:
        copy.wait_send()


def hand_over(*refs):
    src, dst, held = refs[0:4], refs[4:8], refs[8:12]
    sem_in, sem_out = refs[12:14]
    pieces = []
    for i in range(4):
        count = 4 if i < 3 else 2
        rows = src[i].shape[0] // count
        for r in range(count):
            at = pl.ds(r * rows, rows)
            n = len(pieces)
            pieces.append(
                (
                    pltpu.make_async_copy(src[i].at[at], held[i].at[at], sem_in.at[n]),
                    pltpu.make_async_copy(held[i].at[at], dst[i].at[at], sem_out.at[n]),
                )
            )
    for fetch, _ in pieces:
        fetch.start()
    for fetch, put in pieces:
        fetch.wait()
        put.start()
    for _, put in pieces:
        put.wait()


def per_device(q, k, v, g, w, periods, log_decay):
    anywhere = pl.BlockSpec(memory_space=pl.ANY)
    vmem = pl.BlockSpec(memory_space=pltpu.VMEM)
    dma = pltpu.SemaphoreType.DMA
    shapes = (
        jax.ShapeDtypeStruct((ROWS, NH * DK), BF),
        jax.ShapeDtypeStruct((ROWS, NH * DK), BF),
        jax.ShapeDtypeStruct((ROWS, NH * DK), BF),
        jax.ShapeDtypeStruct((HALF, NH * DK), F32),
    )
    made = pl.pallas_call(
        kernel,
        out_shape=shapes,
        in_specs=[pl.BlockSpec(memory_space=pltpu.SMEM), vmem] + [anywhere] * 5,
        out_specs=[vmem] * 4,
        scratch_shapes=[
            pltpu.VMEM((ROWS, 512), BF),
            pltpu.VMEM((ROWS, 512), BF),
            pltpu.VMEM((ROWS, 512), BF),
            pltpu.VMEM((ROWS, 512), BF),
            pltpu.VMEM((8, 2, ROWS, HALF), BF),
            pltpu.VMEM((8, 512, 512), BF),
            pltpu.VMEM((ROWS, 512), F32),
            pltpu.VMEM((8, BLK), F32),
            pltpu.VMEM((8, BLK), F32),
            pltpu.VMEM((8, BLK, DK), F32),
            pltpu.VMEM((8, BLK, DK), F32),
            pltpu.VMEM((8, 3, HALF, HALF), F32),
            pltpu.VMEM((8, 3, HALF, HALF), BF),
            pltpu.VMEM((8, DK, BLK), BF),
            pltpu.VMEM((512, ROWS), BF),
            pltpu.VMEM((8, DK, DK), F32),
            pltpu.VMEM((8, DK, DK), BF),
            pltpu.VMEM((8, DK, DK), F32),
            pltpu.VMEM((ROWS, 512), F32),
            pltpu.VMEM((TM, 40, DK), F32),
            pltpu.VMEM((TM, 40, DK), F32),
            pltpu.VMEM((TM, 32, DK), BF),
            pltpu.VMEM((TM, 32, DK), BF),
            pltpu.VMEM((TM, 32, DK), BF),
            pltpu.VMEM((TM, 32, DK), BF),
            pltpu.VMEM((TM, 32, DK), BF),
            pltpu.VMEM((TM, 32, DK), BF),
            pltpu.VMEM((TM, 8, DK), F32),
            pltpu.VMEM((16, HALF, HALF), BF),
            pltpu.VMEM((16, HALF, HALF), BF),
            pltpu.VMEM((8, HALF, HALF), F32),
            pltpu.VMEM((16, HALF, HALF), BF),
            pltpu.VMEM((2, 4, 2, HALF, HALF), BF),
            pltpu.VMEM((512, HALF), BF),
            pltpu.VMEM((512, HALF), BF),
            dma((6,)),
            dma((18,)),
            dma((18,)),
            dma((15,)),
            dma((15,)),
            dma((64,)),
            dma((64,)),
            dma((16,)),
            dma((16,)),
            dma((16,)),
            dma((2, 4, 2)),
            dma((1,)),
            dma((1,)),
        ],
        compiler_params=pltpu.CompilerParams(
            collective_id=0, has_side_effects=True, vmem_limit_bytes=66_000_000
        ),
    )(periods, log_decay, q, k, v, g, w)
    return pl.pallas_call(
        hand_over,
        out_shape=shapes,
        in_specs=[anywhere] * 4,
        out_specs=[anywhere] * 4,
        scratch_shapes=[pltpu.VMEM(t.shape, t.dtype) for t in shapes] + [dma((14,)), dma((14,))],
    )(*made)


def solution(mesh):
    return jax.shard_map(
        per_device,
        mesh=mesh,
        in_specs=(
            P("tm", "head"),
            P("tm", "head"),
            P("tm", "head"),
            P("tm", "head"),
            P("tm", "head"),
            P("head"),
            P("head", "tm"),
        ),
        out_specs=(P("tm", "head"), P("tm", "head"), P("tm", "head"), P("tm", "head")),
        check_vma=False,
    )
```

```python
import jax
import jax.numpy as jnp
from jax import lax
from jax.experimental import pallas as pl
from jax.experimental.pallas import tpu as pltpu
from jax.sharding import PartitionSpec as P

DK = 128
BLK = 512
NH = 4
TM = 16
ROWS = 1024
HALF = 256
BF = jnp.bfloat16
F32 = jnp.float32
MESH = pl.DeviceIdType.MESH


def mm(a, b):
    return jnp.dot(a, b, preferred_element_type=F32)


def mm_nt(a, b):
    return lax.dot_general(a, b, (((1,), (1,)), ((), ())), preferred_element_type=F32)


def mm_tn(a, b):
    return lax.dot_general(a, b, (((0,), (0,)), ((), ())), preferred_element_type=F32)


def column(row):
    return jnp.transpose(jnp.broadcast_to(row, (DK, row.shape[1])))


def kernel(
    per_ref,
    ld_ref,
    q_hbm,
    k_hbm,
    v_hbm,
    g_hbm,
    w_hbm,
    dq_hbm,
    dk_hbm,
    dv_hbm,
    gw_hbm,
    dq_ref,
    dk_ref,
    dv_ref,
    gw_ref,
    q,
    k,
    v,
    e,
    grads,
    weight,
    acc,
    cum,
    upd,
    fcol,
    ecol,
    mask,
    wts,
    qst,
    mixt,
    st,
    sb,
    rl,
    dvp,
    tx_s,
    rx_s,
    tx_p,
    rx_p,
    tx_r,
    rx_r,
    tx_o,
    rx_o,
    dec,
    pair_tx,
    pair_rx,
    pair_own,
    y_tx,
    y_rx,
    z_tx,
    z_rx,
    out_sem,
    load_sem,
    ag_send,
    ag_recv,
    w_send,
    w_recv,
    s_send,
    s_recv,
    c_send,
    c_recv,
    y_send,
    y_recv,
    z_send,
    z_recv,
):
    tm = lax.axis_index("tm")
    hd = lax.axis_index("head")
    x = lax.rem(hd, 4)
    zh = hd // 4
    right = zh * 4 + lax.rem(x + 1, 4)
    left = zh * 4 + lax.rem(x + 3, 4)
    far = zh * 4 + lax.rem(x + 2, 4)
    across = lax.rem(hd + 4, 8)
    core = lax.rem(tm, 2)
    y = lax.rem(tm // 2, 4)
    zl = tm // 8
    mate = tm + 1 - 2 * core

    def tm_at(zl_, y_, core_):
        return (zl_ * 4 + y_) * 2 + core_

    def local(src, dst, i):
        return pltpu.make_async_copy(src, dst, load_sem.at[i])

    loads = [
        local(k_hbm, k, 0),
        local(v_hbm, v, 1),
        local(q_hbm, q, 2),
        local(g_hbm.at[:, 0:HALF], grads.at[hd, 0], 3),
        local(g_hbm.at[:, HALF:512], grads.at[hd, 1], 4),
        local(w_hbm, weight.at[tm // 2, pl.ds(core * HALF, HALF)], 5),
    ]
    for item in loads:
        item.start()

    barrier = pltpu.get_barrier_semaphore()
    for d in range(1, TM):
        pl.semaphore_signal(
            barrier, inc=1, device_id={"tm": lax.rem(tm + d, TM)}, device_id_type=MESH
        )
    for peer in (right, left, across):
        pl.semaphore_signal(barrier, inc=1, device_id={"head": peer}, device_id_type=MESH)
    ids = lax.broadcasted_iota(jnp.int32, (8, BLK), 0)
    lane = lax.broadcasted_iota(jnp.int32, (8, BLK), 1)
    head_of = lax.rem(ids, NH)
    period = jnp.full((8, BLK), per_ref[0], jnp.int32)
    for h in range(1, NH):
        period = jnp.where(head_of == h, per_ref[h], period)
    period = period.astype(F32)
    pos = (tm * ROWS + (ids // NH) * BLK + lane).astype(F32)
    turns = jnp.floor((pos + 0.5) * (1.0 / period))
    update = jnp.where(pos == turns * period, 1.0, 0.0).astype(F32)
    cum[0:NH, :] = ld_ref[:, 0:BLK]
    cum[NH : 2 * NH, :] = ld_ref[:, BLK : 2 * BLK]
    run = update * period * cum[...]
    shift = 1
    while shift < BLK:
        run = run + jnp.where(lane >= shift, pltpu.roll(run, shift, axis=1), 0.0)
        shift *= 2
    cum[...] = run
    upd[...] = update

    pl.semaphore_wait(barrier, TM + 2)

    sent = []

    def send(src, dst, send_sem, recv_sem, device):
        copy = pltpu.make_async_remote_copy(
            src_ref=src,
            dst_ref=dst,
            send_sem=send_sem,
            recv_sem=recv_sem,
            device_id=device,
            device_id_type=MESH,
        )
        copy.start()
        sent.append(copy)
        return copy

    def gather(src, slot, c, first, count, peer, n):
        rows = pl.ds(first, count)
        if src is g_hbm:
            block = g_hbm.at[:, c * HALF : (c + 1) * HALF]
        else:
            block = grads.at[slot, c]
        return send(
            block.at[rows],
            grads.at[slot, c, rows],
            ag_send.at[n],
            ag_recv.at[n],
            {"head": peer},
        )

    to_right, to_left = [], []
    for c in range(2):
        to_right.append(gather(g_hbm, hd, c, 0, ROWS, right, c))
        to_left.append(gather(g_hbm, hd, c, 0, ROWS, left, 2 + c))
    to_across = [gather(g_hbm, hd, 0, 0, ROWS, across, 4)]

    def w_copy(src, owner, device, n):
        return send(
            src,
            weight.at[owner // 2, pl.ds(lax.rem(owner, 2) * HALF, HALF)],
            w_send.at[n],
            w_recv.at[n],
            {"tm": device},
        )

    def w_block(owner):
        return weight.at[owner // 2, pl.ds(lax.rem(owner, 2) * HALF, HALF)]

    def rows_of(p):
        return cum[pl.ds(p, 1), :], upd[pl.ds(p, 1), :]

    def total_of(p):
        row = cum[pl.ds(p, 1), :]
        return jnp.broadcast_to(row[:, BLK - 1 : BLK], (1, DK))

    def cols(h):
        return pl.ds(pl.multiple_of(h * DK, DK), DK)

    loads[0].wait()
    loads[1].wait()

    @pl.loop(0, NH)
    def _(h):
        for b in range(2):
            p = b * NH + h
            row, urow = rows_of(p)
            factor = column(urow * jnp.exp(row[:, BLK - 1 : BLK] - row))
            fcol[p] = factor
            scaled = (k[b * BLK : (b + 1) * BLK, cols(h)].astype(F32) * factor).astype(BF)
            st[p] = mm_tn(scaled, v[b * BLK : (b + 1) * BLK, cols(h)])
        t0, t1 = total_of(h), total_of(NH + h)
        whole = jnp.exp(t1) * st[h] + st[NH + h]
        for u in range(4):
            tx_s[h * 4 + u, 0:32] = whole[32 * u : 32 * u + 32]
            tx_s[h * 4 + u, 32:40] = jnp.broadcast_to(t0 + t1, (8, DK))

    steps = [(dz, dy, dc) for dz in (1, 0) for dy in (2, 1, 3, 0) for dc in (1, 0)][:-1]

    def exchange(tx, rx, kind):
        copies = []
        for n, (dz, dy, dc) in enumerate(steps):
            peer = tm_at(lax.rem(zl + dz, 2), lax.rem(y + dy, 4), lax.rem(core + dc, 2))
            n = kind * TM + n
            copies.append(
                send(tx.at[peer], rx.at[tm], s_send.at[n], s_recv.at[n], {"tm": peer})
            )
        return copies

    s_first = exchange(tx_s, rx_s, 0)
    rx_s[tm] = tx_s[tm]
    w_across = w_copy(w_hbm, tm, tm_at(1 - zl, y, core), 0)
    w_near = [
        w_copy(w_hbm, tm, tm_at(zl, lax.rem(y + d, 4), core), d) for d in range(1, 4)
    ]
    w_pair = [w_copy(w_hbm, tm, mate, 7)]
    loads[2].wait()

    @pl.loop(0, NH)
    def _(h):
        low = lax.broadcasted_iota(jnp.int32, (HALF, HALF), 0) >= lax.broadcasted_iota(
            jnp.int32, (HALF, HALF), 1
        )
        for b in range(2):
            p = b * NH + h
            row, urow = rows_of(p)
            at = column(row)
            grown = jnp.exp(at)
            ecol[p] = grown
            qb = q[b * BLK : (b + 1) * BLK, cols(h)]
            kb = k[b * BLK : (b + 1) * BLK, cols(h)]
            qst[p] = jnp.transpose(qb.astype(F32) * grown).astype(BF)
            wide = jnp.concatenate([at, at], axis=1)
            for n, (ti, si) in enumerate(((0, 0), (1, 0), (1, 1))):
                gap = wide[ti * HALF : (ti + 1) * HALF] - row[:, si * HALF : (si + 1) * HALF]
                if ti == si:
                    gap = jnp.where(low, gap, -jnp.inf)
                tile = jnp.exp(gap) * urow[:, si * HALF : (si + 1) * HALF]
                mask[p, n] = tile
                score = mm_nt(qb[ti * HALF : (ti + 1) * HALF], kb[si * HALF : (si + 1) * HALF])
                wts[p, n] = (tile * score).astype(BF)

    for copy in s_first:
        copy.wait_recv()
    part = jnp.zeros((32, DK), F32)
    for i in range(TM):
        tx_p[i] = part.astype(BF)
        fall = jnp.exp(rx_s[i, 32:40])
        dec[i] = fall
        part = jnp.concatenate([fall] * 4, axis=0) * part + rx_s[i, 0:32]
    s_second = exchange(tx_p, rx_p, 1)
    rx_p[tm] = tx_p[tm]
    to_across.append(gather(g_hbm, hd, 1, 0, ROWS, across, 5))

    on_right, on_left = [], []

    def pass_x(c):
        to_right[c].wait_recv()
        on_right.append(gather(grads, left, c, 0, 512, right, 6 + c))
        to_left[c].wait_recv()
        on_left.append(gather(grads, right, c, 512, 512, left, 8 + c))

    p_right, p_left = [], []

    def pass_z(c):
        to_across[c].wait_recv()
        p_right.append(gather(grads, across, c, 0, ROWS, right, 10 + c))
        p_left.append(gather(grads, across, c, 0, ROWS, left, 12 + c))

    on_across = []

    def pass_far(c):
        on_right[c].wait_recv()
        on_across.append(gather(grads, far, c, 0, 512, across, 14 + 2 * c))
        on_left[c].wait_recv()
        on_across.append(gather(grads, far, c, 512, 512, across, 15 + 2 * c))

    pass_x(0)
    w_across.wait_recv()
    z_mate = tm_at(1 - zl, y, core)
    w_far = [
        w_copy(w_block(z_mate), z_mate, tm_at(zl, lax.rem(y + d, 4), core), 3 + d)
        for d in range(1, 4)
    ]
    w_pair.append(w_copy(w_block(z_mate), z_mate, mate, 8))

    for copy in s_second:
        copy.wait_recv()

    @pl.loop(0, NH)
    def _(h):
        start = rx_p[pl.ds(h * 4, 4)].reshape(DK, DK).astype(F32)
        starts = (start, jnp.exp(total_of(h)) * start + st[h])
        for b in range(2):
            p = b * NH + h
            state = starts[b].astype(BF)
            sb[p] = state
            rows = slice(b * BLK, (b + 1) * BLK)
            v0 = v[b * BLK : b * BLK + HALF, cols(h)]
            v1 = v[b * BLK + HALF : (b + 1) * BLK, cols(h)]
            within = jnp.concatenate(
                [mm(wts[p, 0], v0), mm(wts[p, 1], v0) + mm(wts[p, 2], v1)], axis=0
            )
            mixed = within + ecol[p] * mm(q[rows, cols(h)], state)
            mixt[cols(h), rows] = jnp.transpose(mixed).astype(BF)

    @pl.loop(0, 4)
    def _(r):
        acc[pl.ds(r * HALF, HALF), :] = jnp.zeros((HALF, NH * DK), F32)

    def w_rows(s, c):
        return weight[s, c * HALF : (c + 1) * HALF, :]

    def grow_mixed(*units, last=False):
        @pl.loop(0, 4)
        def _(r):
            rows = pl.ds(pl.multiple_of(r * HALF, HALF), HALF)
            total = acc[rows, :]
            for s, c in units:
                total = total + mm(grads[s, c, rows, :], w_rows(s, c))
            if last:
                e[rows, :] = total.astype(BF)
            else:
                acc[rows, :] = total

    mine = pl.ds(pl.multiple_of(core * HALF, HALF), HALF)
    other = pl.ds(pl.multiple_of((1 - core) * HALF, HALF), HALF)
    units = []
    pairs = []
    y_sent = []

    def grow_weight(s, c):
        n = len(units)
        units.append((s, c))
        pair_tx[n] = mm(mixt[other, :], grads[s, c]).astype(BF)
        pairs.append(
            send(pair_tx.at[n], pair_rx.at[n], c_send.at[n], c_recv.at[n], {"tm": mate})
        )
        pair_own[n % 8] = mm(mixt[mine, :], grads[s, c])

    def add_pairs():
        for n in range(len(y_sent), len(units)):
            s, c = units[n]
            pairs[n].wait_recv()
            y_tx[n] = (pair_own[n % 8] + pair_rx[n].astype(F32)).astype(BF)
            gap = lax.rem(lax.rem(s, 4) + 4 - y, 4)
            part_z = s // 4
            copy = pltpu.make_async_remote_copy(
                src_ref=y_tx.at[n],
                dst_ref=y_rx.at[part_z, y, core],
                send_sem=y_send.at[n],
                recv_sem=y_recv.at[part_z, gap, core],
                device_id={"tm": tm_at(zl, lax.rem(s, 4), c)},
                device_id_type=MESH,
            )
            away = jnp.logical_or(gap != 0, core != c)

            @pl.when(away)
            def _():
                copy.start()

            @pl.when(jnp.logical_not(away))
            def _():
                y_rx[part_z, y, core] = y_tx[n]

            y_sent.append((away, copy))

    z_right = lax.rem(right + 4, 8)
    z_left = lax.rem(left + 4, 8)
    z_far = lax.rem(far + 4, 8)

    loads[3].wait()
    loads[4].wait()
    grow_weight(hd, 0)
    grow_weight(hd, 1)
    pass_x(1)
    pass_z(0)
    add_pairs()
    for c in range(2):
        grow_weight(left, c)
        grow_weight(right, c)
    for d in range(1, 4):
        src = tm_at(zl, lax.rem(y + 4 - d, 4), core)
        w_near[d - 1].wait_recv()
        w_pair.append(w_copy(w_block(src), src, mate, 8 + d))
    add_pairs()
    pass_far(0)
    grow_weight(across, 0)
    grow_weight(far, 0)
    pass_z(1)
    add_pairs()
    grow_weight(across, 1)
    for d in range(1, 4):
        src = tm_at(1 - zl, lax.rem(y + 4 - d, 4), core)
        w_far[d - 1].wait_recv()
        w_pair.append(w_copy(w_block(src), src, mate, 11 + d))
    pass_far(1)
    grow_weight(far, 1)
    add_pairs()
    loads[5].wait()
    for copy in w_pair:
        copy.wait_recv()
    grow_mixed(*units[0:5])
    grow_mixed(*units[5:10])
    for copy in (p_right[0], p_left[0], on_across[0], on_across[1]):
        copy.wait_recv()
    grow_weight(z_left, 0)
    grow_weight(z_right, 0)
    grow_weight(z_far, 0)
    grow_mixed(*units[10:13])
    add_pairs()
    for copy in (on_across[2], on_across[3]):
        copy.wait_recv()
    grow_weight(z_far, 1)
    grow_mixed(units[13])
    add_pairs()
    def y_arrivals(part_z):
        def arrive(gap, half):
            pltpu.make_async_remote_copy(
                src_ref=y_tx.at[0],
                dst_ref=y_rx.at[0, 0, 0],
                send_sem=y_send.at[0],
                recv_sem=y_recv.at[part_z, gap, half],
                device_id={"tm": mate},
                device_id_type=MESH,
            ).wait_recv()

        for gap in range(1, 4):
            for half in range(2):
                arrive(gap, half)
        arrive(0, 1 - core)

    def y_sum(part_z, half):
        total = y_rx[part_z, 0, half].astype(F32)
        for i in range(1, 4):
            total = total + y_rx[part_z, i, half].astype(F32)
        return total

    z_copy = pltpu.make_async_remote_copy(
        src_ref=z_tx,
        dst_ref=z_rx,
        send_sem=z_send.at[0],
        recv_sem=z_recv.at[0],
        device_id={"tm": z_mate},
        device_id_type=MESH,
    )
    sent.append(z_copy)

    def z_stage():
        y_arrivals(1 - zl)
        for r in range(2):
            z_tx[r * HALF : (r + 1) * HALF, :] = y_sum(1 - zl, r).astype(BF)
        z_copy.start()

    @pl.when(core == 0)
    def _():
        z_stage()

    p_right[1].wait_recv()
    p_left[1].wait_recv()
    grow_mixed((z_left, 1), (z_right, 1), last=True)

    @pl.loop(0, NH)
    def _(h):
        for b in range(2):
            rl[b * NH + h] = mm(qst[b * NH + h], e[b * BLK : (b + 1) * BLK, cols(h)])
        whole = jnp.exp(total_of(h)) * rl[NH + h] + rl[h]
        for u in range(4):
            tx_r[h * 4 + u] = whole[32 * u : 32 * u + 32].astype(BF)

    r_first = exchange(tx_r, rx_r, 2)
    rx_r[tm] = tx_r[tm]
    grow_weight(z_left, 1)
    grow_weight(z_right, 1)
    add_pairs()

    def local_grads(h):
        for b in range(2):
            p = b * NH + h
            rows = slice(b * BLK, (b + 1) * BLK)
            eb = e[rows, cols(h)]
            qb = q[rows, cols(h)]
            kb = k[rows, cols(h)]
            vb = v[rows, cols(h)]
            lo, hi = slice(0, HALF), slice(HALF, BLK)
            bk = []
            for n, (ti, si) in enumerate(((lo, lo), (hi, lo), (hi, hi))):
                bk.append((mask[p, n] * mm_nt(eb[ti], vb[si])).astype(BF))
            near = jnp.concatenate(
                [mm(bk[0], kb[lo]), mm(bk[1], kb[lo]) + mm(bk[2], kb[hi])], axis=0
            )
            dq_ref[rows, cols(h)] = (near + ecol[p] * mm_nt(eb, sb[p])).astype(BF)
            acc[b * BLK : b * BLK + HALF, cols(h)] = mm_tn(bk[0], qb[lo]) + mm_tn(bk[1], qb[hi])
            acc[b * BLK + HALF : (b + 1) * BLK, cols(h)] = mm_tn(bk[2], qb[hi])
            dvp[b * BLK : b * BLK + HALF, cols(h)] = mm_tn(wts[p, 0], eb[lo]) + mm_tn(
                wts[p, 1], eb[hi]
            )
            dvp[b * BLK + HALF : (b + 1) * BLK, cols(h)] = mm_tn(wts[p, 2], eb[hi])

    @pl.loop(0, 2)
    def _(h):
        local_grads(h)

    for copy in r_first:
        copy.wait_recv()
    part = jnp.zeros((32, DK), F32)
    for i in reversed(range(TM)):
        tx_o[i] = part.astype(BF)
        part = jnp.concatenate([dec[i]] * 4, axis=0) * part + rx_r[i].astype(F32)
    r_second = exchange(tx_o, rx_o, 3)
    rx_o[tm] = tx_o[tm]

    results = [
        pltpu.make_async_copy(held, out, out_sem.at[i])
        for i, (held, out) in enumerate(
            ((dq_ref, dq_hbm), (dk_ref, dk_hbm), (dv_ref, dv_hbm), (gw_ref, gw_hbm))
        )
    ]
    @pl.loop(2, NH)
    def _(h):
        local_grads(h)

    results[0].start()
    @pl.when(core == 1)
    def _():
        z_stage()

    y_arrivals(zl)
    for r in range(2):
        pair_own[r] = y_sum(zl, r)
    for copy in r_second:
        copy.wait_recv()

    @pl.loop(0, NH)
    def _(h):
        end = rx_o[pl.ds(h * 4, 4)].reshape(DK, DK).astype(F32)
        ends = (jnp.exp(total_of(NH + h)) * end + rl[NH + h], end)
        for b in range(2):
            p = b * NH + h
            rows = slice(b * BLK, (b + 1) * BLK)
            carried = ends[b].astype(BF)
            dk_ref[rows, cols(h)] = (
                acc[rows, cols(h)] + fcol[p] * mm_nt(v[rows, cols(h)], carried)
            ).astype(BF)
            dv_ref[rows, cols(h)] = (
                dvp[rows, cols(h)] + fcol[p] * mm(k[rows, cols(h)], carried)
            ).astype(BF)

    results[1].start()
    results[2].start()
    z_copy.wait_recv()
    for r in range(2):
        rows = slice(r * HALF, (r + 1) * HALF)
        total = pair_own[r] + z_rx[rows, :].astype(F32)
        gw_ref[:, rows] = jnp.transpose(total)
    results[3].start()

    for away, copy in y_sent:

        @pl.when(away)
        def _():
            copy.wait_send()

    for copy in sent:
        copy.wait_send()
    for copy in results:
        copy.wait()


def hand_over(*refs):
    src, dst, held = refs[0:4], refs[4:8], refs[8:12]
    sem_in, sem_out = refs[12:14]
    pieces = []
    for i in range(4):
        count = 4 if i < 3 else 2
        rows = src[i].shape[0] // count
        for r in range(count):
            at = pl.ds(r * rows, rows)
            n = len(pieces)
            pieces.append(
                (
                    pltpu.make_async_copy(src[i].at[at], held[i].at[at], sem_in.at[n]),
                    pltpu.make_async_copy(held[i].at[at], dst[i].at[at], sem_out.at[n]),
                )
            )
    for fetch, _ in pieces:
        fetch.start()
    for fetch, put in pieces:
        fetch.wait()
        put.start()
    for _, put in pieces:
        put.wait()


def per_device(q, k, v, g, w, periods, log_decay):
    anywhere = pl.BlockSpec(memory_space=pl.ANY)
    vmem = pl.BlockSpec(memory_space=pltpu.VMEM)
    dma = pltpu.SemaphoreType.DMA
    shapes = (
        jax.ShapeDtypeStruct((ROWS, NH * DK), BF),
        jax.ShapeDtypeStruct((ROWS, NH * DK), BF),
        jax.ShapeDtypeStruct((ROWS, NH * DK), BF),
        jax.ShapeDtypeStruct((HALF, NH * DK), F32),
    )
    made = pl.pallas_call(
        kernel,
        out_shape=shapes,
        in_specs=[pl.BlockSpec(memory_space=pltpu.SMEM), vmem] + [anywhere] * 5,
        out_specs=[anywhere] * 4,
        scratch_shapes=[pltpu.VMEM(t.shape, t.dtype) for t in shapes]
        + [
            pltpu.VMEM((ROWS, 512), BF),
            pltpu.VMEM((ROWS, 512), BF),
            pltpu.VMEM((ROWS, 512), BF),
            pltpu.VMEM((ROWS, 512), BF),
            pltpu.VMEM((8, 2, ROWS, HALF), BF),
            pltpu.VMEM((8, 512, 512), BF),
            pltpu.VMEM((ROWS, 512), F32),
            pltpu.VMEM((8, BLK), F32),
            pltpu.VMEM((8, BLK), F32),
            pltpu.VMEM((8, BLK, DK), F32),
            pltpu.VMEM((8, BLK, DK), F32),
            pltpu.VMEM((8, 3, HALF, HALF), F32),
            pltpu.VMEM((8, 3, HALF, HALF), BF),
            pltpu.VMEM((8, DK, BLK), BF),
            pltpu.VMEM((512, ROWS), BF),
            pltpu.VMEM((8, DK, DK), F32),
            pltpu.VMEM((8, DK, DK), BF),
            pltpu.VMEM((8, DK, DK), F32),
            pltpu.VMEM((ROWS, 512), F32),
            pltpu.VMEM((TM, 40, DK), F32),
            pltpu.VMEM((TM, 40, DK), F32),
            pltpu.VMEM((TM, 32, DK), BF),
            pltpu.VMEM((TM, 32, DK), BF),
            pltpu.VMEM((TM, 32, DK), BF),
            pltpu.VMEM((TM, 32, DK), BF),
            pltpu.VMEM((TM, 32, DK), BF),
            pltpu.VMEM((TM, 32, DK), BF),
            pltpu.VMEM((TM, 8, DK), F32),
            pltpu.VMEM((16, HALF, HALF), BF),
            pltpu.VMEM((16, HALF, HALF), BF),
            pltpu.VMEM((8, HALF, HALF), F32),
            pltpu.VMEM((16, HALF, HALF), BF),
            pltpu.VMEM((2, 4, 2, HALF, HALF), BF),
            pltpu.VMEM((512, HALF), BF),
            pltpu.VMEM((512, HALF), BF),
            dma((4,)),
            dma((6,)),
            dma((18,)),
            dma((18,)),
            dma((15,)),
            dma((15,)),
            dma((64,)),
            dma((64,)),
            dma((16,)),
            dma((16,)),
            dma((16,)),
            dma((2, 4, 2)),
            dma((1,)),
            dma((1,)),
        ],
        compiler_params=pltpu.CompilerParams(
            collective_id=0, has_side_effects=True, vmem_limit_bytes=66_000_000
        ),
    )(periods, log_decay, q, k, v, g, w)
    return pl.pallas_call(
        hand_over,
        out_shape=shapes,
        in_specs=[anywhere] * 4,
        out_specs=[anywhere] * 4,
        scratch_shapes=[pltpu.VMEM(t.shape, t.dtype) for t in shapes] + [dma((14,)), dma((14,))],
    )(*made)


def solution(mesh):
    return jax.shard_map(
        per_device,
        mesh=mesh,
        in_specs=(
            P("tm", "head"),
            P("tm", "head"),
            P("tm", "head"),
            P("tm", "head"),
            P("tm", "head"),
            P("head"),
            P("head", "tm"),
        ),
        out_specs=(P("tm", "head"), P("tm", "head"), P("tm", "head"), P("tm", "head")),
        check_vma=False,
    )
```

```python
import jax
import jax.numpy as jnp
from jax import lax
from jax.experimental import pallas as pl
from jax.experimental.pallas import tpu as pltpu
from jax.sharding import PartitionSpec as P

DK = 128
BLK = 512
NH = 4
TM = 16
ROWS = 1024
HALF = 256
BF = jnp.bfloat16
F32 = jnp.float32
MESH = pl.DeviceIdType.MESH


def mm(a, b):
    return jnp.dot(a, b, preferred_element_type=F32)


def mm_nt(a, b):
    return lax.dot_general(a, b, (((1,), (1,)), ((), ())), preferred_element_type=F32)


def mm_tn(a, b):
    return lax.dot_general(a, b, (((0,), (0,)), ((), ())), preferred_element_type=F32)


def column(row):
    return jnp.transpose(jnp.broadcast_to(row, (DK, row.shape[1])))


def kernel(
    per_ref,
    ld_ref,
    q_hbm,
    k_hbm,
    v_hbm,
    g_hbm,
    w_hbm,
    dq_hbm,
    dk_hbm,
    dv_hbm,
    gw_hbm,
    dq_ref,
    dk_ref,
    dv_ref,
    gw_ref,
    q,
    k,
    v,
    e,
    grads,
    weight,
    acc,
    cum,
    upd,
    fcol,
    ecol,
    mask,
    wts,
    qst,
    mixt,
    st,
    sb,
    rl,
    dvp,
    tx_s,
    rx_s,
    tx_p,
    rx_p,
    tx_r,
    rx_r,
    tx_o,
    rx_o,
    dec,
    pair_tx,
    pair_rx,
    pair_own,
    y_tx,
    y_rx,
    z_tx,
    z_rx,
    out_sem,
    load_sem,
    ag_send,
    ag_recv,
    w_send,
    w_recv,
    s_send,
    s_recv,
    c_send,
    c_recv,
    y_send,
    y_recv,
    z_send,
    z_recv,
):
    tm = lax.axis_index("tm")
    hd = lax.axis_index("head")
    x = lax.rem(hd, 4)
    zh = hd // 4
    right = zh * 4 + lax.rem(x + 1, 4)
    left = zh * 4 + lax.rem(x + 3, 4)
    far = zh * 4 + lax.rem(x + 2, 4)
    across = lax.rem(hd + 4, 8)
    core = lax.rem(tm, 2)
    y = lax.rem(tm // 2, 4)
    zl = tm // 8
    mate = tm + 1 - 2 * core

    def tm_at(zl_, y_, core_):
        return (zl_ * 4 + y_) * 2 + core_

    def local(src, dst, i):
        return pltpu.make_async_copy(src, dst, load_sem.at[i])

    loads = [
        local(k_hbm, k, 0),
        local(v_hbm, v, 1),
        local(q_hbm, q, 2),
        local(g_hbm.at[:, 0:HALF], grads.at[hd, 0], 3),
        local(g_hbm.at[:, HALF:512], grads.at[hd, 1], 4),
        local(w_hbm, weight.at[tm // 2, pl.ds(core * HALF, HALF)], 5),
    ]
    for item in loads:
        item.start()

    barrier = pltpu.get_barrier_semaphore()
    for d in range(1, TM):
        pl.semaphore_signal(
            barrier, inc=1, device_id={"tm": lax.rem(tm + d, TM)}, device_id_type=MESH
        )
    for peer in (right, left, across):
        pl.semaphore_signal(barrier, inc=1, device_id={"head": peer}, device_id_type=MESH)
    ids = lax.broadcasted_iota(jnp.int32, (8, BLK), 0)
    lane = lax.broadcasted_iota(jnp.int32, (8, BLK), 1)
    head_of = lax.rem(ids, NH)
    period = jnp.full((8, BLK), per_ref[0], jnp.int32)
    for h in range(1, NH):
        period = jnp.where(head_of == h, per_ref[h], period)
    period = period.astype(F32)
    pos = (tm * ROWS + (ids // NH) * BLK + lane).astype(F32)
    turns = jnp.floor((pos + 0.5) * (1.0 / period))
    update = jnp.where(pos == turns * period, 1.0, 0.0).astype(F32)
    cum[0:NH, :] = ld_ref[:, 0:BLK]
    cum[NH : 2 * NH, :] = ld_ref[:, BLK : 2 * BLK]
    run = update * period * cum[...]
    shift = 1
    while shift < BLK:
        run = run + jnp.where(lane >= shift, pltpu.roll(run, shift, axis=1), 0.0)
        shift *= 2
    cum[...] = run
    upd[...] = update

    pl.semaphore_wait(barrier, TM + 2)

    sent = []

    def send(src, dst, send_sem, recv_sem, device):
        copy = pltpu.make_async_remote_copy(
            src_ref=src,
            dst_ref=dst,
            send_sem=send_sem,
            recv_sem=recv_sem,
            device_id=device,
            device_id_type=MESH,
        )
        copy.start()
        sent.append(copy)
        return copy

    def gather(src, slot, c, first, count, peer, n):
        rows = pl.ds(first, count)
        if src is g_hbm:
            block = g_hbm.at[:, c * HALF : (c + 1) * HALF]
        else:
            block = grads.at[slot, c]
        return send(
            block.at[rows],
            grads.at[slot, c, rows],
            ag_send.at[n],
            ag_recv.at[n],
            {"head": peer},
        )

    to_right, to_left = [], []
    for c in range(2):
        to_right.append(gather(g_hbm, hd, c, 0, ROWS, right, c))
        to_left.append(gather(g_hbm, hd, c, 0, ROWS, left, 2 + c))
    to_across = [gather(g_hbm, hd, 0, 0, ROWS, across, 4)]

    def w_copy(src, owner, device, n):
        return send(
            src,
            weight.at[owner // 2, pl.ds(lax.rem(owner, 2) * HALF, HALF)],
            w_send.at[n],
            w_recv.at[n],
            {"tm": device},
        )

    def w_block(owner):
        return weight.at[owner // 2, pl.ds(lax.rem(owner, 2) * HALF, HALF)]

    def rows_of(p):
        return cum[pl.ds(p, 1), :], upd[pl.ds(p, 1), :]

    def total_of(p):
        row = cum[pl.ds(p, 1), :]
        return jnp.broadcast_to(row[:, BLK - 1 : BLK], (1, DK))

    def cols(h):
        return pl.ds(pl.multiple_of(h * DK, DK), DK)

    loads[0].wait()
    loads[1].wait()

    @pl.loop(0, NH)
    def _(h):
        for b in range(2):
            p = b * NH + h
            row, urow = rows_of(p)
            factor = column(urow * jnp.exp(row[:, BLK - 1 : BLK] - row))
            fcol[p] = factor
            scaled = (k[b * BLK : (b + 1) * BLK, cols(h)].astype(F32) * factor).astype(BF)
            st[p] = mm_tn(scaled, v[b * BLK : (b + 1) * BLK, cols(h)])
        t0, t1 = total_of(h), total_of(NH + h)
        whole = jnp.exp(t1) * st[h] + st[NH + h]
        for u in range(4):
            tx_s[h * 4 + u, 0:32] = whole[32 * u : 32 * u + 32]
            tx_s[h * 4 + u, 32:40] = jnp.broadcast_to(t0 + t1, (8, DK))

    steps = [(dz, dy, dc) for dz in (1, 0) for dy in (2, 1, 3, 0) for dc in (1, 0)][:-1]

    def exchange(tx, rx, kind):
        copies = []
        for n, (dz, dy, dc) in enumerate(steps):
            peer = tm_at(lax.rem(zl + dz, 2), lax.rem(y + dy, 4), lax.rem(core + dc, 2))
            n = kind * TM + n
            copies.append(
                send(tx.at[peer], rx.at[tm], s_send.at[n], s_recv.at[n], {"tm": peer})
            )
        return copies

    s_first = exchange(tx_s, rx_s, 0)
    rx_s[tm] = tx_s[tm]
    w_across = w_copy(w_hbm, tm, tm_at(1 - zl, y, core), 0)
    w_near = [
        w_copy(w_hbm, tm, tm_at(zl, lax.rem(y + d, 4), core), d) for d in range(1, 4)
    ]
    w_pair = [w_copy(w_hbm, tm, mate, 7)]
    loads[2].wait()

    @pl.loop(0, NH)
    def _(h):
        low = lax.broadcasted_iota(jnp.int32, (HALF, HALF), 0) >= lax.broadcasted_iota(
            jnp.int32, (HALF, HALF), 1
        )
        for b in range(2):
            p = b * NH + h
            row, urow = rows_of(p)
            at = column(row)
            grown = jnp.exp(at)
            ecol[p] = grown
            qb = q[b * BLK : (b + 1) * BLK, cols(h)]
            kb = k[b * BLK : (b + 1) * BLK, cols(h)]
            qst[p] = jnp.transpose(qb.astype(F32) * grown).astype(BF)
            wide = jnp.concatenate([at, at], axis=1)
            for n, (ti, si) in enumerate(((0, 0), (1, 0), (1, 1))):
                gap = wide[ti * HALF : (ti + 1) * HALF] - row[:, si * HALF : (si + 1) * HALF]
                if ti == si:
                    gap = jnp.where(low, gap, -jnp.inf)
                tile = jnp.exp(gap) * urow[:, si * HALF : (si + 1) * HALF]
                mask[p, n] = tile
                score = mm_nt(qb[ti * HALF : (ti + 1) * HALF], kb[si * HALF : (si + 1) * HALF])
                wts[p, n] = (tile * score).astype(BF)

    for copy in s_first:
        copy.wait_recv()
    part = jnp.zeros((32, DK), F32)
    for i in range(TM):
        tx_p[i] = part.astype(BF)
        fall = jnp.exp(rx_s[i, 32:40])
        dec[i] = fall
        part = jnp.concatenate([fall] * 4, axis=0) * part + rx_s[i, 0:32]
    s_second = exchange(tx_p, rx_p, 1)
    rx_p[tm] = tx_p[tm]
    to_across.append(gather(g_hbm, hd, 1, 0, ROWS, across, 5))

    on_right, on_left = [], []

    def pass_x(c):
        to_right[c].wait_recv()
        on_right.append(gather(grads, left, c, 0, 512, right, 6 + c))
        to_left[c].wait_recv()
        on_left.append(gather(grads, right, c, 512, 512, left, 8 + c))

    p_right, p_left = [], []

    def quarter(slot, sub, peer, n):
        block = grads.at[slot, 1, :, sub * DK : (sub + 1) * DK]
        return send(block, block, ag_send.at[n], ag_recv.at[n], {"head": peer})

    def pass_z(c):
        to_across[c].wait_recv()
        if c == 0:
            p_right.append(gather(grads, across, c, 0, ROWS, right, 10))
            p_left.append(gather(grads, across, c, 0, ROWS, left, 12))
        else:
            for sub in range(2):
                p_right.append(quarter(across, sub, right, 18 + sub))
                p_left.append(quarter(across, sub, left, 20 + sub))

    on_across = []

    def pass_far(c):
        on_right[c].wait_recv()
        on_across.append(gather(grads, far, c, 0, 512, across, 14 + 2 * c))
        on_left[c].wait_recv()
        on_across.append(gather(grads, far, c, 512, 512, across, 15 + 2 * c))

    pass_x(0)
    w_across.wait_recv()
    z_mate = tm_at(1 - zl, y, core)
    w_far = [
        w_copy(w_block(z_mate), z_mate, tm_at(zl, lax.rem(y + d, 4), core), 3 + d)
        for d in range(1, 4)
    ]
    w_pair.append(w_copy(w_block(z_mate), z_mate, mate, 8))

    for copy in s_second:
        copy.wait_recv()

    @pl.loop(0, NH)
    def _(h):
        start = rx_p[pl.ds(h * 4, 4)].reshape(DK, DK).astype(F32)
        starts = (start, jnp.exp(total_of(h)) * start + st[h])
        for b in range(2):
            p = b * NH + h
            state = starts[b].astype(BF)
            sb[p] = state
            rows = slice(b * BLK, (b + 1) * BLK)
            v0 = v[b * BLK : b * BLK + HALF, cols(h)]
            v1 = v[b * BLK + HALF : (b + 1) * BLK, cols(h)]
            within = jnp.concatenate(
                [mm(wts[p, 0], v0), mm(wts[p, 1], v0) + mm(wts[p, 2], v1)], axis=0
            )
            mixed = within + ecol[p] * mm(q[rows, cols(h)], state)
            mixt[cols(h), rows] = jnp.transpose(mixed).astype(BF)

    @pl.loop(0, 4)
    def _(r):
        acc[pl.ds(r * HALF, HALF), :] = jnp.zeros((HALF, NH * DK), F32)

    def w_rows(s, c):
        return weight[s, c * HALF : (c + 1) * HALF, :]

    def grow_mixed(*units):
        @pl.loop(0, 4)
        def _(r):
            rows = pl.ds(pl.multiple_of(r * HALF, HALF), HALF)
            total = acc[rows, :]
            for s, c in units:
                total = total + mm(grads[s, c, rows, :], w_rows(s, c))
            acc[rows, :] = total

    mine = pl.ds(pl.multiple_of(core * HALF, HALF), HALF)
    other = pl.ds(pl.multiple_of((1 - core) * HALF, HALF), HALF)
    units = []
    pairs = []
    y_sent = []

    def grow_weight(s, c):
        n = len(units)
        units.append((s, c))
        pair_tx[n] = mm(mixt[other, :], grads[s, c]).astype(BF)
        pairs.append(
            send(pair_tx.at[n], pair_rx.at[n], c_send.at[n], c_recv.at[n], {"tm": mate})
        )
        pair_own[n % 8] = mm(mixt[mine, :], grads[s, c])

    def y_put(s, c, m, sub):
        gap = lax.rem(lax.rem(s, 4) + 4 - y, 4)
        part_z = s // 4
        at = pl.ds(sub * DK, DK) if c else pl.ds(0, HALF)
        copy = pltpu.make_async_remote_copy(
            src_ref=y_tx.at[m, :, at],
            dst_ref=y_rx.at[part_z, y, core, :, at],
            send_sem=y_send.at[2 * m + sub],
            recv_sem=y_recv.at[part_z, gap, core, sub],
            device_id={"tm": tm_at(zl, lax.rem(s, 4), c)},
            device_id_type=MESH,
        )
        away = jnp.logical_or(gap != 0, core != c)

        @pl.when(away)
        def _():
            copy.start()

        @pl.when(jnp.logical_not(away))
        def _():
            y_rx[part_z, y, core, :, at] = y_tx[m, :, at]

        y_sent.append((away, copy))

    added = []

    def add_pairs():
        for n in range(len(added), len(units)):
            s, c = units[n]
            pairs[n].wait_recv()
            y_tx[n] = (pair_own[n % 8] + pair_rx[n].astype(F32)).astype(BF)
            for sub in range(1 + c):
                y_put(s, c, n, sub)
            added.append(n)

    def last_weight(sub):
        at = pl.ds(sub * DK, DK)
        block = jnp.concatenate([grads[z_left, 1, :, at], grads[z_right, 1, :, at]], axis=1)
        part = mm(mixt[other, :], block).astype(BF)
        copies = []
        for i in range(2):
            m, n = 14 + i, 14 + 2 * sub + i
            pair_tx[m, :, at] = part[:, i * DK : (i + 1) * DK]
            copies.append(
                send(
                    pair_tx.at[m, :, at],
                    pair_rx.at[m, :, at],
                    c_send.at[n],
                    c_recv.at[n],
                    {"tm": mate},
                )
            )
        part = mm(mixt[mine, :], block)
        for i in range(2):
            pair_own[6 + i, :, at] = part[:, i * DK : (i + 1) * DK]
        return copies

    def last_add(sub, copies):
        at = pl.ds(sub * DK, DK)
        for i, s in enumerate((z_left, z_right)):
            copies[i].wait_recv()
            y_tx[14 + i, :, at] = (
                pair_own[6 + i, :, at] + pair_rx[14 + i, :, at].astype(F32)
            ).astype(BF)
            y_put(s, 1, 14 + i, sub)

    def last_mixed(sub, dst):
        at = pl.ds(sub * DK, DK)
        deep = pl.ds(HALF + sub * DK, DK)
        block = jnp.concatenate([weight[z_left, deep, :], weight[z_right, deep, :]], axis=0)

        @pl.loop(0, 4)
        def _(r):
            rows = pl.ds(pl.multiple_of(r * HALF, HALF), HALF)
            held = jnp.concatenate(
                [grads[z_left, 1, rows, at], grads[z_right, 1, rows, at]], axis=1
            )
            dst[rows, :] = (acc[rows, :] + mm(held, block)).astype(dst.dtype)

    z_right = lax.rem(right + 4, 8)
    z_left = lax.rem(left + 4, 8)
    z_far = lax.rem(far + 4, 8)

    loads[3].wait()
    loads[4].wait()
    grow_weight(hd, 0)
    grow_weight(hd, 1)
    pass_x(1)
    pass_z(0)
    add_pairs()
    for c in range(2):
        grow_weight(left, c)
        grow_weight(right, c)
    for d in range(1, 4):
        src = tm_at(zl, lax.rem(y + 4 - d, 4), core)
        w_near[d - 1].wait_recv()
        w_pair.append(w_copy(w_block(src), src, mate, 8 + d))
    add_pairs()
    pass_far(0)
    grow_weight(across, 0)
    grow_weight(far, 0)
    pass_z(1)
    add_pairs()
    grow_weight(across, 1)
    for d in range(1, 4):
        src = tm_at(1 - zl, lax.rem(y + 4 - d, 4), core)
        w_far[d - 1].wait_recv()
        w_pair.append(w_copy(w_block(src), src, mate, 11 + d))
    pass_far(1)
    grow_weight(far, 1)
    add_pairs()
    loads[5].wait()
    for copy in w_pair:
        copy.wait_recv()
    grow_mixed(*units[0:5])
    grow_mixed(*units[5:10])
    for copy in (p_right[0], p_left[0], on_across[0], on_across[1]):
        copy.wait_recv()
    grow_weight(z_left, 0)
    grow_weight(z_right, 0)
    grow_weight(z_far, 0)
    grow_mixed(*units[10:13])
    add_pairs()
    for copy in (on_across[2], on_across[3]):
        copy.wait_recv()
    grow_weight(z_far, 1)
    grow_mixed(units[13])
    add_pairs()
    def y_arrivals(part_z, c, subs):
        def arrive(gap, half, sub):
            at = pl.ds(sub * DK, DK) if c else pl.ds(0, HALF)
            pltpu.make_async_remote_copy(
                src_ref=y_tx.at[0, :, at],
                dst_ref=y_rx.at[0, 0, 0, :, at],
                send_sem=y_send.at[0],
                recv_sem=y_recv.at[part_z, gap, half, sub],
                device_id={"tm": mate},
                device_id_type=MESH,
            ).wait_recv()

        for sub in subs:
            for gap in range(1, 4):
                for half in range(2):
                    arrive(gap, half, sub)
            arrive(0, 1 - c, sub)

    def y_sum(part_z, half, at=slice(None)):
        total = y_rx[part_z, 0, half, :, at].astype(F32)
        for i in range(1, 4):
            total = total + y_rx[part_z, i, half, :, at].astype(F32)
        return total

    z_copies = []
    for sub in range(2):
        at = pl.ds(sub * DK, DK)
        z_copies.append(
            pltpu.make_async_remote_copy(
                src_ref=z_tx.at[:, at],
                dst_ref=z_rx.at[:, at],
                send_sem=z_send.at[sub],
                recv_sem=z_recv.at[sub],
                device_id={"tm": z_mate},
                device_id_type=MESH,
            )
        )
    sent.extend(z_copies)

    def z_stage(c, subs):
        y_arrivals(1 - zl, c, subs if c else (0,))
        for sub in subs:
            at = pl.ds(sub * DK, DK)
            for r in range(2):
                z_tx[r * HALF : (r + 1) * HALF, at] = y_sum(1 - zl, r, at).astype(BF)
            z_copies[sub].start()

    p_right[1].wait_recv()
    p_left[1].wait_recv()
    first_quarter = last_weight(0)
    last_mixed(0, acc)
    last_add(0, first_quarter)

    @pl.when(core == 0)
    def _():
        z_stage(0, (0, 1))

    p_right[2].wait_recv()
    p_left[2].wait_recv()
    last_mixed(1, e)

    @pl.loop(0, NH)
    def _(h):
        for b in range(2):
            rl[b * NH + h] = mm(qst[b * NH + h], e[b * BLK : (b + 1) * BLK, cols(h)])
        whole = jnp.exp(total_of(h)) * rl[NH + h] + rl[h]
        for u in range(4):
            tx_r[h * 4 + u] = whole[32 * u : 32 * u + 32].astype(BF)

    r_first = exchange(tx_r, rx_r, 2)
    rx_r[tm] = tx_r[tm]
    last_add(1, last_weight(1))

    def local_grads(h):
        for b in range(2):
            p = b * NH + h
            rows = slice(b * BLK, (b + 1) * BLK)
            eb = e[rows, cols(h)]
            qb = q[rows, cols(h)]
            kb = k[rows, cols(h)]
            vb = v[rows, cols(h)]
            lo, hi = slice(0, HALF), slice(HALF, BLK)
            bk = []
            for n, (ti, si) in enumerate(((lo, lo), (hi, lo), (hi, hi))):
                bk.append((mask[p, n] * mm_nt(eb[ti], vb[si])).astype(BF))
            near = jnp.concatenate(
                [mm(bk[0], kb[lo]), mm(bk[1], kb[lo]) + mm(bk[2], kb[hi])], axis=0
            )
            dq_ref[rows, cols(h)] = (near + ecol[p] * mm_nt(eb, sb[p])).astype(BF)
            acc[b * BLK : b * BLK + HALF, cols(h)] = mm_tn(bk[0], qb[lo]) + mm_tn(bk[1], qb[hi])
            acc[b * BLK + HALF : (b + 1) * BLK, cols(h)] = mm_tn(bk[2], qb[hi])
            dvp[b * BLK : b * BLK + HALF, cols(h)] = mm_tn(wts[p, 0], eb[lo]) + mm_tn(
                wts[p, 1], eb[hi]
            )
            dvp[b * BLK + HALF : (b + 1) * BLK, cols(h)] = mm_tn(wts[p, 2], eb[hi])

    @pl.loop(0, 2)
    def _(h):
        local_grads(h)

    @pl.when(core == 1)
    def _():
        z_stage(1, (0,))

    for copy in r_first:
        copy.wait_recv()
    part = jnp.zeros((32, DK), F32)
    for i in reversed(range(TM)):
        tx_o[i] = part.astype(BF)
        part = jnp.concatenate([dec[i]] * 4, axis=0) * part + rx_r[i].astype(F32)
    r_second = exchange(tx_o, rx_o, 3)
    rx_o[tm] = tx_o[tm]

    results = [
        pltpu.make_async_copy(held, out, out_sem.at[i])
        for i, (held, out) in enumerate(
            ((dq_ref, dq_hbm), (dk_ref, dk_hbm), (dv_ref, dv_hbm), (gw_ref, gw_hbm))
        )
    ]
    @pl.loop(2, NH)
    def _(h):
        local_grads(h)

    results[0].start()

    @pl.when(core == 1)
    def _():
        z_stage(1, (1,))
        y_arrivals(zl, 1, (0, 1))

    @pl.when(core == 0)
    def _():
        y_arrivals(zl, 0, (0,))

    for r in range(2):
        pair_own[r] = y_sum(zl, r)
    for copy in r_second:
        copy.wait_recv()

    @pl.loop(0, NH)
    def _(h):
        end = rx_o[pl.ds(h * 4, 4)].reshape(DK, DK).astype(F32)
        ends = (jnp.exp(total_of(NH + h)) * end + rl[NH + h], end)
        for b in range(2):
            p = b * NH + h
            rows = slice(b * BLK, (b + 1) * BLK)
            carried = ends[b].astype(BF)
            dk_ref[rows, cols(h)] = (
                acc[rows, cols(h)] + fcol[p] * mm_nt(v[rows, cols(h)], carried)
            ).astype(BF)
            dv_ref[rows, cols(h)] = (
                dvp[rows, cols(h)] + fcol[p] * mm(k[rows, cols(h)], carried)
            ).astype(BF)

    results[1].start()
    results[2].start()
    for copy in z_copies:
        copy.wait_recv()
    for r in range(2):
        rows = slice(r * HALF, (r + 1) * HALF)
        total = pair_own[r] + z_rx[rows, :].astype(F32)
        gw_ref[:, rows] = jnp.transpose(total)
    results[3].start()

    for away, copy in y_sent:

        @pl.when(away)
        def _():
            copy.wait_send()

    for copy in sent:
        copy.wait_send()
    for copy in results:
        copy.wait()


def hand_over(*refs):
    src, dst, held = refs[0:4], refs[4:8], refs[8:12]
    sem_in, sem_out = refs[12:14]
    pieces = []
    for i in range(4):
        count = 4 if i < 3 else 2
        rows = src[i].shape[0] // count
        for r in range(count):
            at = pl.ds(r * rows, rows)
            n = len(pieces)
            pieces.append(
                (
                    pltpu.make_async_copy(src[i].at[at], held[i].at[at], sem_in.at[n]),
                    pltpu.make_async_copy(held[i].at[at], dst[i].at[at], sem_out.at[n]),
                )
            )
    for fetch, _ in pieces:
        fetch.start()
    for fetch, put in pieces:
        fetch.wait()
        put.start()
    for _, put in pieces:
        put.wait()


def per_device(q, k, v, g, w, periods, log_decay):
    anywhere = pl.BlockSpec(memory_space=pl.ANY)
    vmem = pl.BlockSpec(memory_space=pltpu.VMEM)
    dma = pltpu.SemaphoreType.DMA
    shapes = (
        jax.ShapeDtypeStruct((ROWS, NH * DK), BF),
        jax.ShapeDtypeStruct((ROWS, NH * DK), BF),
        jax.ShapeDtypeStruct((ROWS, NH * DK), BF),
        jax.ShapeDtypeStruct((HALF, NH * DK), F32),
    )
    made = pl.pallas_call(
        kernel,
        out_shape=shapes,
        in_specs=[pl.BlockSpec(memory_space=pltpu.SMEM), vmem] + [anywhere] * 5,
        out_specs=[anywhere] * 4,
        scratch_shapes=[pltpu.VMEM(t.shape, t.dtype) for t in shapes]
        + [
            pltpu.VMEM((ROWS, 512), BF),
            pltpu.VMEM((ROWS, 512), BF),
            pltpu.VMEM((ROWS, 512), BF),
            pltpu.VMEM((ROWS, 512), BF),
            pltpu.VMEM((8, 2, ROWS, HALF), BF),
            pltpu.VMEM((8, 512, 512), BF),
            pltpu.VMEM((ROWS, 512), F32),
            pltpu.VMEM((8, BLK), F32),
            pltpu.VMEM((8, BLK), F32),
            pltpu.VMEM((8, BLK, DK), F32),
            pltpu.VMEM((8, BLK, DK), F32),
            pltpu.VMEM((8, 3, HALF, HALF), F32),
            pltpu.VMEM((8, 3, HALF, HALF), BF),
            pltpu.VMEM((8, DK, BLK), BF),
            pltpu.VMEM((512, ROWS), BF),
            pltpu.VMEM((8, DK, DK), F32),
            pltpu.VMEM((8, DK, DK), BF),
            pltpu.VMEM((8, DK, DK), F32),
            pltpu.VMEM((ROWS, 512), F32),
            pltpu.VMEM((TM, 40, DK), F32),
            pltpu.VMEM((TM, 40, DK), F32),
            pltpu.VMEM((TM, 32, DK), BF),
            pltpu.VMEM((TM, 32, DK), BF),
            pltpu.VMEM((TM, 32, DK), BF),
            pltpu.VMEM((TM, 32, DK), BF),
            pltpu.VMEM((TM, 32, DK), BF),
            pltpu.VMEM((TM, 32, DK), BF),
            pltpu.VMEM((TM, 8, DK), F32),
            pltpu.VMEM((16, HALF, HALF), BF),
            pltpu.VMEM((16, HALF, HALF), BF),
            pltpu.VMEM((8, HALF, HALF), F32),
            pltpu.VMEM((16, HALF, HALF), BF),
            pltpu.VMEM((2, 4, 2, HALF, HALF), BF),
            pltpu.VMEM((512, HALF), BF),
            pltpu.VMEM((512, HALF), BF),
            dma((4,)),
            dma((6,)),
            dma((22,)),
            dma((22,)),
            dma((15,)),
            dma((15,)),
            dma((64,)),
            dma((64,)),
            dma((18,)),
            dma((18,)),
            dma((32,)),
            dma((2, 4, 2, 2)),
            dma((2,)),
            dma((2,)),
        ],
        compiler_params=pltpu.CompilerParams(
            collective_id=0, has_side_effects=True, vmem_limit_bytes=66_000_000
        ),
    )(periods, log_decay, q, k, v, g, w)
    return pl.pallas_call(
        hand_over,
        out_shape=shapes,
        in_specs=[anywhere] * 4,
        out_specs=[anywhere] * 4,
        scratch_shapes=[pltpu.VMEM(t.shape, t.dtype) for t in shapes] + [dma((14,)), dma((14,))],
    )(*made)


def solution(mesh):
    return jax.shard_map(
        per_device,
        mesh=mesh,
        in_specs=(
            P("tm", "head"),
            P("tm", "head"),
            P("tm", "head"),
            P("tm", "head"),
            P("tm", "head"),
            P("head"),
            P("head", "tm"),
        ),
        out_specs=(P("tm", "head"), P("tm", "head"), P("tm", "head"), P("tm", "head")),
        check_vma=False,
    )
```

```python
import jax
import jax.numpy as jnp
from jax import lax
from jax.experimental import pallas as pl
from jax.experimental.pallas import tpu as pltpu
from jax.sharding import PartitionSpec as P

DK = 128
BLK = 512
NH = 4
TM = 16
ROWS = 1024
HALF = 256
BF = jnp.bfloat16
F32 = jnp.float32
MESH = pl.DeviceIdType.MESH


def mm(a, b):
    return jnp.dot(a, b, preferred_element_type=F32)


def mm_nt(a, b):
    return lax.dot_general(a, b, (((1,), (1,)), ((), ())), preferred_element_type=F32)


def mm_tn(a, b):
    return lax.dot_general(a, b, (((0,), (0,)), ((), ())), preferred_element_type=F32)


def column(row):
    return jnp.transpose(jnp.broadcast_to(row, (DK, row.shape[1])))


def kernel(
    per_ref,
    ld_ref,
    q_hbm,
    k_hbm,
    v_hbm,
    g_hbm,
    w_hbm,
    dq_hbm,
    dk_hbm,
    dv_hbm,
    gw_hbm,
    dq_ref,
    dk_ref,
    dv_ref,
    gw_ref,
    q,
    k,
    v,
    e,
    grads,
    weight,
    acc,
    cum,
    upd,
    fcol,
    ecol,
    mask,
    wts,
    qst,
    mixt,
    st,
    sb,
    rl,
    dvp,
    tx_s,
    rx_s,
    tx_p,
    rx_p,
    tx_r,
    rx_r,
    tx_o,
    rx_o,
    dec,
    pair_tx,
    pair_rx,
    pair_own,
    y_tx,
    y_rx,
    z_tx,
    z_rx,
    out_sem,
    load_sem,
    ag_send,
    ag_recv,
    w_send,
    w_recv,
    s_send,
    s_recv,
    c_send,
    c_recv,
    y_send,
    y_recv,
    z_send,
    z_recv,
):
    tm = lax.axis_index("tm")
    hd = lax.axis_index("head")
    x = lax.rem(hd, 4)
    zh = hd // 4
    right = zh * 4 + lax.rem(x + 1, 4)
    left = zh * 4 + lax.rem(x + 3, 4)
    far = zh * 4 + lax.rem(x + 2, 4)
    across = lax.rem(hd + 4, 8)
    core = lax.rem(tm, 2)
    y = lax.rem(tm // 2, 4)
    zl = tm // 8
    mate = tm + 1 - 2 * core

    def tm_at(zl_, y_, core_):
        return (zl_ * 4 + y_) * 2 + core_

    def local(src, dst, i):
        return pltpu.make_async_copy(src, dst, load_sem.at[i])

    loads = [
        local(k_hbm, k, 0),
        local(v_hbm, v, 1),
        local(q_hbm, q, 2),
        local(g_hbm.at[:, 0:HALF], grads.at[hd, 0], 3),
        local(g_hbm.at[:, HALF:512], grads.at[hd, 1], 4),
        local(w_hbm, weight.at[tm // 2, pl.ds(core * HALF, HALF)], 5),
    ]
    for item in loads:
        item.start()

    barrier = pltpu.get_barrier_semaphore()
    for d in range(1, TM):
        pl.semaphore_signal(
            barrier, inc=1, device_id={"tm": lax.rem(tm + d, TM)}, device_id_type=MESH
        )
    for peer in (right, left, across):
        pl.semaphore_signal(barrier, inc=1, device_id={"head": peer}, device_id_type=MESH)
    ids = lax.broadcasted_iota(jnp.int32, (8, BLK), 0)
    lane = lax.broadcasted_iota(jnp.int32, (8, BLK), 1)
    head_of = lax.rem(ids, NH)
    period = jnp.full((8, BLK), per_ref[0], jnp.int32)
    for h in range(1, NH):
        period = jnp.where(head_of == h, per_ref[h], period)
    period = period.astype(F32)
    pos = (tm * ROWS + (ids // NH) * BLK + lane).astype(F32)
    turns = jnp.floor((pos + 0.5) * (1.0 / period))
    update = jnp.where(pos == turns * period, 1.0, 0.0).astype(F32)
    cum[0:NH, :] = ld_ref[:, 0:BLK]
    cum[NH : 2 * NH, :] = ld_ref[:, BLK : 2 * BLK]
    run = update * period * cum[...]
    shift = 1
    while shift < BLK:
        run = run + jnp.where(lane >= shift, pltpu.roll(run, shift, axis=1), 0.0)
        shift *= 2
    cum[...] = run
    upd[...] = update

    pl.semaphore_wait(barrier, TM + 2)

    sent = []

    def send(src, dst, send_sem, recv_sem, device):
        copy = pltpu.make_async_remote_copy(
            src_ref=src,
            dst_ref=dst,
            send_sem=send_sem,
            recv_sem=recv_sem,
            device_id=device,
            device_id_type=MESH,
        )
        copy.start()
        sent.append(copy)
        return copy

    def gather(src, slot, c, first, count, peer, n):
        rows = pl.ds(first, count)
        if src is g_hbm:
            block = g_hbm.at[:, c * HALF : (c + 1) * HALF]
        else:
            block = grads.at[slot, c]
        return send(
            block.at[rows],
            grads.at[slot, c, rows],
            ag_send.at[n],
            ag_recv.at[n],
            {"head": peer},
        )

    to_right, to_left = [], []
    for c in range(2):
        to_right.append(gather(g_hbm, hd, c, 0, ROWS, right, c))
        to_left.append(gather(g_hbm, hd, c, 0, ROWS, left, 2 + c))
    to_across = [gather(g_hbm, hd, 0, 0, ROWS, across, 4)]

    def w_copy(src, owner, device, n):
        return send(
            src,
            weight.at[owner // 2, pl.ds(lax.rem(owner, 2) * HALF, HALF)],
            w_send.at[n],
            w_recv.at[n],
            {"tm": device},
        )

    def w_block(owner):
        return weight.at[owner // 2, pl.ds(lax.rem(owner, 2) * HALF, HALF)]

    def rows_of(p):
        return cum[pl.ds(p, 1), :], upd[pl.ds(p, 1), :]

    def total_of(p):
        row = cum[pl.ds(p, 1), :]
        return jnp.broadcast_to(row[:, BLK - 1 : BLK], (1, DK))

    def cols(h):
        return pl.ds(pl.multiple_of(h * DK, DK), DK)

    loads[0].wait()
    loads[1].wait()

    @pl.loop(0, NH)
    def _(h):
        for b in range(2):
            p = b * NH + h
            row, urow = rows_of(p)
            factor = column(urow * jnp.exp(row[:, BLK - 1 : BLK] - row))
            fcol[p] = factor
            scaled = (k[b * BLK : (b + 1) * BLK, cols(h)].astype(F32) * factor).astype(BF)
            st[p] = mm_tn(scaled, v[b * BLK : (b + 1) * BLK, cols(h)])
        t0, t1 = total_of(h), total_of(NH + h)
        whole = jnp.exp(t1) * st[h] + st[NH + h]
        for u in range(4):
            tx_s[h * 4 + u, 0:32] = whole[32 * u : 32 * u + 32]
            tx_s[h * 4 + u, 32:40] = jnp.broadcast_to(t0 + t1, (8, DK))

    steps = [(dz, dy, dc) for dz in (1, 0) for dy in (2, 1, 3, 0) for dc in (1, 0)][:-1]

    def exchange(tx, rx, kind):
        copies = []
        for n, (dz, dy, dc) in enumerate(steps):
            peer = tm_at(lax.rem(zl + dz, 2), lax.rem(y + dy, 4), lax.rem(core + dc, 2))
            n = kind * TM + n
            copies.append(
                send(tx.at[peer], rx.at[tm], s_send.at[n], s_recv.at[n], {"tm": peer})
            )
        return copies

    s_first = exchange(tx_s, rx_s, 0)
    rx_s[tm] = tx_s[tm]
    w_across = w_copy(w_hbm, tm, tm_at(1 - zl, y, core), 0)
    w_near = [
        w_copy(w_hbm, tm, tm_at(zl, lax.rem(y + d, 4), core), d) for d in range(1, 4)
    ]
    w_pair = [w_copy(w_hbm, tm, mate, 7)]
    loads[2].wait()

    @pl.loop(0, NH)
    def _(h):
        low = lax.broadcasted_iota(jnp.int32, (HALF, HALF), 0) >= lax.broadcasted_iota(
            jnp.int32, (HALF, HALF), 1
        )
        for b in range(2):
            p = b * NH + h
            row, urow = rows_of(p)
            at = column(row)
            grown = jnp.exp(at)
            ecol[p] = grown
            qb = q[b * BLK : (b + 1) * BLK, cols(h)]
            kb = k[b * BLK : (b + 1) * BLK, cols(h)]
            qst[p] = jnp.transpose(qb.astype(F32) * grown).astype(BF)
            wide = jnp.concatenate([at, at], axis=1)
            for n, (ti, si) in enumerate(((0, 0), (1, 0), (1, 1))):
                gap = wide[ti * HALF : (ti + 1) * HALF] - row[:, si * HALF : (si + 1) * HALF]
                if ti == si:
                    gap = jnp.where(low, gap, -jnp.inf)
                tile = jnp.exp(gap) * urow[:, si * HALF : (si + 1) * HALF]
                mask[p, n] = tile
                score = mm_nt(qb[ti * HALF : (ti + 1) * HALF], kb[si * HALF : (si + 1) * HALF])
                wts[p, n] = (tile * score).astype(BF)

    for copy in s_first:
        copy.wait_recv()
    part = jnp.zeros((32, DK), F32)
    for i in range(TM):
        tx_p[i] = part.astype(BF)
        fall = jnp.exp(rx_s[i, 32:40])
        dec[i] = fall
        part = jnp.concatenate([fall] * 4, axis=0) * part + rx_s[i, 0:32]
    s_second = exchange(tx_p, rx_p, 1)
    rx_p[tm] = tx_p[tm]
    to_across.append(gather(g_hbm, hd, 1, 0, ROWS, across, 5))

    on_right, on_left = [], []

    def pass_x(c):
        to_right[c].wait_recv()
        on_right.append(gather(grads, left, c, 0, 512, right, 6 + c))
        to_left[c].wait_recv()
        on_left.append(gather(grads, right, c, 512, 512, left, 8 + c))

    p_right, p_left = [], []

    def pass_z(c):
        to_across[c].wait_recv()
        p_right.append(gather(grads, across, c, 0, ROWS, right, 10 + c))
        p_left.append(gather(grads, across, c, 0, ROWS, left, 12 + c))

    on_across = []

    def pass_far(c):
        on_right[c].wait_recv()
        on_across.append(gather(grads, far, c, 0, 512, across, 14 + 2 * c))
        on_left[c].wait_recv()
        on_across.append(gather(grads, far, c, 512, 512, across, 15 + 2 * c))

    pass_x(0)
    w_across.wait_recv()
    z_mate = tm_at(1 - zl, y, core)
    w_far = [
        w_copy(w_block(z_mate), z_mate, tm_at(zl, lax.rem(y + d, 4), core), 3 + d)
        for d in range(1, 4)
    ]
    w_pair.append(w_copy(w_block(z_mate), z_mate, mate, 8))

    pass_x(1)
    pass_z(0)

    for copy in s_second:
        copy.wait_recv()

    @pl.loop(0, NH)
    def _(h):
        start = rx_p[pl.ds(h * 4, 4)].reshape(DK, DK).astype(F32)
        starts = (start, jnp.exp(total_of(h)) * start + st[h])
        for b in range(2):
            p = b * NH + h
            state = starts[b].astype(BF)
            sb[p] = state
            rows = slice(b * BLK, (b + 1) * BLK)
            v0 = v[b * BLK : b * BLK + HALF, cols(h)]
            v1 = v[b * BLK + HALF : (b + 1) * BLK, cols(h)]
            within = jnp.concatenate(
                [mm(wts[p, 0], v0), mm(wts[p, 1], v0) + mm(wts[p, 2], v1)], axis=0
            )
            mixed = within + ecol[p] * mm(q[rows, cols(h)], state)
            mixt[cols(h), rows] = jnp.transpose(mixed).astype(BF)

    @pl.loop(0, 4)
    def _(r):
        acc[pl.ds(r * HALF, HALF), :] = jnp.zeros((HALF, NH * DK), F32)

    def w_rows(s, c):
        return weight[s, c * HALF : (c + 1) * HALF, :]

    def grow_mixed(*units, last=False):
        @pl.loop(0, 4)
        def _(r):
            rows = pl.ds(pl.multiple_of(r * HALF, HALF), HALF)
            total = acc[rows, :]
            for s, c in units:
                total = total + mm(grads[s, c, rows, :], w_rows(s, c))
            if last:
                e[rows, :] = total.astype(BF)
            else:
                acc[rows, :] = total

    mine = pl.ds(pl.multiple_of(core * HALF, HALF), HALF)
    other = pl.ds(pl.multiple_of((1 - core) * HALF, HALF), HALF)
    units = []
    pairs = []
    y_sent = []

    def grow_weight(s, c):
        n = len(units)
        units.append((s, c))
        pair_tx[n] = mm(mixt[other, :], grads[s, c]).astype(BF)
        pairs.append(
            send(pair_tx.at[n], pair_rx.at[n], c_send.at[n], c_recv.at[n], {"tm": mate})
        )
        pair_own[n % 8] = mm(mixt[mine, :], grads[s, c])

    def add_pairs():
        for n in range(len(y_sent), len(units)):
            s, c = units[n]
            pairs[n].wait_recv()
            y_tx[n] = (pair_own[n % 8] + pair_rx[n].astype(F32)).astype(BF)
            gap = lax.rem(lax.rem(s, 4) + 4 - y, 4)
            part_z = s // 4
            copy = pltpu.make_async_remote_copy(
                src_ref=y_tx.at[n],
                dst_ref=y_rx.at[part_z, y, core],
                send_sem=y_send.at[n],
                recv_sem=y_recv.at[part_z, gap, core],
                device_id={"tm": tm_at(zl, lax.rem(s, 4), c)},
                device_id_type=MESH,
            )
            away = jnp.logical_or(gap != 0, core != c)

            @pl.when(away)
            def _():
                copy.start()

            @pl.when(jnp.logical_not(away))
            def _():
                y_rx[part_z, y, core] = y_tx[n]

            y_sent.append((away, copy))

    z_right = lax.rem(right + 4, 8)
    z_left = lax.rem(left + 4, 8)
    z_far = lax.rem(far + 4, 8)

    loads[3].wait()
    loads[4].wait()
    grow_weight(hd, 0)
    grow_weight(hd, 1)
    add_pairs()
    for c in range(2):
        grow_weight(left, c)
        grow_weight(right, c)
    add_pairs()
    pass_far(0)
    pass_z(1)
    for d in range(1, 4):
        src = tm_at(zl, lax.rem(y + 4 - d, 4), core)
        w_near[d - 1].wait_recv()
        w_pair.append(w_copy(w_block(src), src, mate, 8 + d))
    grow_weight(across, 0)
    grow_weight(far, 0)
    add_pairs()
    grow_weight(across, 1)
    pass_far(1)
    for d in range(1, 4):
        src = tm_at(1 - zl, lax.rem(y + 4 - d, 4), core)
        w_far[d - 1].wait_recv()
        w_pair.append(w_copy(w_block(src), src, mate, 11 + d))
    grow_weight(far, 1)
    add_pairs()
    loads[5].wait()
    for copy in w_pair:
        copy.wait_recv()
    grow_mixed(*units[0:5])
    grow_mixed(*units[5:10])
    for copy in (p_right[0], p_left[0], on_across[0], on_across[1]):
        copy.wait_recv()
    grow_weight(z_left, 0)
    grow_weight(z_right, 0)
    grow_weight(z_far, 0)
    grow_mixed(*units[10:13])
    add_pairs()
    for copy in (on_across[2], on_across[3]):
        copy.wait_recv()
    grow_weight(z_far, 1)
    grow_mixed(units[13])
    add_pairs()
    def y_arrivals(part_z):
        def arrive(gap, half):
            pltpu.make_async_remote_copy(
                src_ref=y_tx.at[0],
                dst_ref=y_rx.at[0, 0, 0],
                send_sem=y_send.at[0],
                recv_sem=y_recv.at[part_z, gap, half],
                device_id={"tm": mate},
                device_id_type=MESH,
            ).wait_recv()

        for gap in range(1, 4):
            for half in range(2):
                arrive(gap, half)
        arrive(0, 1 - core)

    def y_sum(part_z, half):
        total = y_rx[part_z, 0, half].astype(F32)
        for i in range(1, 4):
            total = total + y_rx[part_z, i, half].astype(F32)
        return total

    z_copy = pltpu.make_async_remote_copy(
        src_ref=z_tx,
        dst_ref=z_rx,
        send_sem=z_send.at[0],
        recv_sem=z_recv.at[0],
        device_id={"tm": z_mate},
        device_id_type=MESH,
    )
    sent.append(z_copy)

    def z_stage():
        y_arrivals(1 - zl)
        for r in range(2):
            z_tx[r * HALF : (r + 1) * HALF, :] = y_sum(1 - zl, r).astype(BF)
        z_copy.start()

    @pl.when(core == 0)
    def _():
        z_stage()

    p_right[1].wait_recv()
    p_left[1].wait_recv()
    grow_mixed((z_left, 1), (z_right, 1), last=True)

    @pl.loop(0, NH)
    def _(h):
        for b in range(2):
            rl[b * NH + h] = mm(qst[b * NH + h], e[b * BLK : (b + 1) * BLK, cols(h)])
        whole = jnp.exp(total_of(h)) * rl[NH + h] + rl[h]
        for u in range(4):
            tx_r[h * 4 + u] = whole[32 * u : 32 * u + 32].astype(BF)

    r_first = exchange(tx_r, rx_r, 2)
    rx_r[tm] = tx_r[tm]
    grow_weight(z_left, 1)
    grow_weight(z_right, 1)

    def local_grads(h):
        for b in range(2):
            p = b * NH + h
            rows = slice(b * BLK, (b + 1) * BLK)
            eb = e[rows, cols(h)]
            qb = q[rows, cols(h)]
            kb = k[rows, cols(h)]
            vb = v[rows, cols(h)]
            lo, hi = slice(0, HALF), slice(HALF, BLK)
            bk = []
            for n, (ti, si) in enumerate(((lo, lo), (hi, lo), (hi, hi))):
                bk.append((mask[p, n] * mm_nt(eb[ti], vb[si])).astype(BF))
            near = jnp.concatenate(
                [mm(bk[0], kb[lo]), mm(bk[1], kb[lo]) + mm(bk[2], kb[hi])], axis=0
            )
            dq_ref[rows, cols(h)] = (near + ecol[p] * mm_nt(eb, sb[p])).astype(BF)
            acc[b * BLK : b * BLK + HALF, cols(h)] = mm_tn(bk[0], qb[lo]) + mm_tn(bk[1], qb[hi])
            acc[b * BLK + HALF : (b + 1) * BLK, cols(h)] = mm_tn(bk[2], qb[hi])
            dvp[b * BLK : b * BLK + HALF, cols(h)] = mm_tn(wts[p, 0], eb[lo]) + mm_tn(
                wts[p, 1], eb[hi]
            )
            dvp[b * BLK + HALF : (b + 1) * BLK, cols(h)] = mm_tn(wts[p, 2], eb[hi])

    @pl.loop(0, 1)
    def _(h):
        local_grads(h)

    add_pairs()

    @pl.loop(1, 2)
    def _(h):
        local_grads(h)

    for copy in r_first:
        copy.wait_recv()
    part = jnp.zeros((32, DK), F32)
    for i in reversed(range(TM)):
        tx_o[i] = part.astype(BF)
        part = jnp.concatenate([dec[i]] * 4, axis=0) * part + rx_r[i].astype(F32)
    r_second = exchange(tx_o, rx_o, 3)
    rx_o[tm] = tx_o[tm]

    results = [
        pltpu.make_async_copy(held, out, out_sem.at[i])
        for i, (held, out) in enumerate(
            ((dq_ref, dq_hbm), (dk_ref, dk_hbm), (dv_ref, dv_hbm), (gw_ref, gw_hbm))
        )
    ]
    @pl.loop(2, NH)
    def _(h):
        local_grads(h)

    results[0].start()
    @pl.when(core == 1)
    def _():
        z_stage()

    y_arrivals(zl)
    for r in range(2):
        pair_own[r] = y_sum(zl, r)
    for copy in r_second:
        copy.wait_recv()

    @pl.loop(0, NH)
    def _(h):
        end = rx_o[pl.ds(h * 4, 4)].reshape(DK, DK).astype(F32)
        ends = (jnp.exp(total_of(NH + h)) * end + rl[NH + h], end)
        for b in range(2):
            p = b * NH + h
            rows = slice(b * BLK, (b + 1) * BLK)
            carried = ends[b].astype(BF)
            dk_ref[rows, cols(h)] = (
                acc[rows, cols(h)] + fcol[p] * mm_nt(v[rows, cols(h)], carried)
            ).astype(BF)
            dv_ref[rows, cols(h)] = (
                dvp[rows, cols(h)] + fcol[p] * mm(k[rows, cols(h)], carried)
            ).astype(BF)

    results[1].start()
    results[2].start()
    z_copy.wait_recv()
    for r in range(2):
        rows = slice(r * HALF, (r + 1) * HALF)
        total = pair_own[r] + z_rx[rows, :].astype(F32)
        gw_ref[:, rows] = jnp.transpose(total)
    results[3].start()

    for away, copy in y_sent:

        @pl.when(away)
        def _():
            copy.wait_send()

    for copy in sent:
        copy.wait_send()
    for copy in results:
        copy.wait()


def hand_over(*refs):
    src, dst, held = refs[0:4], refs[4:8], refs[8:12]
    sem_in, sem_out = refs[12:14]
    pieces = []
    for i in range(4):
        count = 4 if i < 3 else 2
        rows = src[i].shape[0] // count
        for r in range(count):
            at = pl.ds(r * rows, rows)
            n = len(pieces)
            pieces.append(
                (
                    pltpu.make_async_copy(src[i].at[at], held[i].at[at], sem_in.at[n]),
                    pltpu.make_async_copy(held[i].at[at], dst[i].at[at], sem_out.at[n]),
                )
            )
    for fetch, _ in pieces:
        fetch.start()
    for fetch, put in pieces:
        fetch.wait()
        put.start()
    for _, put in pieces:
        put.wait()


def per_device(q, k, v, g, w, periods, log_decay):
    anywhere = pl.BlockSpec(memory_space=pl.ANY)
    vmem = pl.BlockSpec(memory_space=pltpu.VMEM)
    dma = pltpu.SemaphoreType.DMA
    shapes = (
        jax.ShapeDtypeStruct((ROWS, NH * DK), BF),
        jax.ShapeDtypeStruct((ROWS, NH * DK), BF),
        jax.ShapeDtypeStruct((ROWS, NH * DK), BF),
        jax.ShapeDtypeStruct((HALF, NH * DK), F32),
    )
    made = pl.pallas_call(
        kernel,
        out_shape=shapes,
        in_specs=[pl.BlockSpec(memory_space=pltpu.SMEM), vmem] + [anywhere] * 5,
        out_specs=[anywhere] * 4,
        scratch_shapes=[pltpu.VMEM(t.shape, t.dtype) for t in shapes]
        + [
            pltpu.VMEM((ROWS, 512), BF),
            pltpu.VMEM((ROWS, 512), BF),
            pltpu.VMEM((ROWS, 512), BF),
            pltpu.VMEM((ROWS, 512), BF),
            pltpu.VMEM((8, 2, ROWS, HALF), BF),
            pltpu.VMEM((8, 512, 512), BF),
            pltpu.VMEM((ROWS, 512), F32),
            pltpu.VMEM((8, BLK), F32),
            pltpu.VMEM((8, BLK), F32),
            pltpu.VMEM((8, BLK, DK), F32),
            pltpu.VMEM((8, BLK, DK), F32),
            pltpu.VMEM((8, 3, HALF, HALF), F32),
            pltpu.VMEM((8, 3, HALF, HALF), BF),
            pltpu.VMEM((8, DK, BLK), BF),
            pltpu.VMEM((512, ROWS), BF),
            pltpu.VMEM((8, DK, DK), F32),
            pltpu.VMEM((8, DK, DK), BF),
            pltpu.VMEM((8, DK, DK), F32),
            pltpu.VMEM((ROWS, 512), F32),
            pltpu.VMEM((TM, 40, DK), F32),
            pltpu.VMEM((TM, 40, DK), F32),
            pltpu.VMEM((TM, 32, DK), BF),
            pltpu.VMEM((TM, 32, DK), BF),
            pltpu.VMEM((TM, 32, DK), BF),
            pltpu.VMEM((TM, 32, DK), BF),
            pltpu.VMEM((TM, 32, DK), BF),
            pltpu.VMEM((TM, 32, DK), BF),
            pltpu.VMEM((TM, 8, DK), F32),
            pltpu.VMEM((16, HALF, HALF), BF),
            pltpu.VMEM((16, HALF, HALF), BF),
            pltpu.VMEM((8, HALF, HALF), F32),
            pltpu.VMEM((16, HALF, HALF), BF),
            pltpu.VMEM((2, 4, 2, HALF, HALF), BF),
            pltpu.VMEM((512, HALF), BF),
            pltpu.VMEM((512, HALF), BF),
            dma((4,)),
            dma((6,)),
            dma((18,)),
            dma((18,)),
            dma((15,)),
            dma((15,)),
            dma((64,)),
            dma((64,)),
            dma((16,)),
            dma((16,)),
            dma((16,)),
            dma((2, 4, 2)),
            dma((1,)),
            dma((1,)),
        ],
        compiler_params=pltpu.CompilerParams(
            collective_id=0, has_side_effects=True, vmem_limit_bytes=66_000_000
        ),
    )(periods, log_decay, q, k, v, g, w)
    return pl.pallas_call(
        hand_over,
        out_shape=shapes,
        in_specs=[anywhere] * 4,
        out_specs=[anywhere] * 4,
        scratch_shapes=[pltpu.VMEM(t.shape, t.dtype) for t in shapes] + [dma((14,)), dma((14,))],
    )(*made)


def solution(mesh):
    return jax.shard_map(
        per_device,
        mesh=mesh,
        in_specs=(
            P("tm", "head"),
            P("tm", "head"),
            P("tm", "head"),
            P("tm", "head"),
            P("tm", "head"),
            P("head"),
            P("head", "tm"),
        ),
        out_specs=(P("tm", "head"), P("tm", "head"), P("tm", "head"), P("tm", "head")),
        check_vma=False,
    )
```
